128 devices in a mesh: leaf: 16 (over y, x), front: 8 (over z, core).
Axes of the slice: x: 4, y: 4, z: 4, core: 2. Of those that a mesh axis runs over, the one named last changes fastest.
Arguments:
- rhs: bfloat16 [3, 16384, 256], P(None, ('leaf', 'front')), may hold values from -6 to 6
- inverse_blocks: bfloat16 [16384, 7168], P(('leaf', 'front')), may hold values from -0.125 to 0.125
- update_blocks: bfloat16 [16384, 3072], P(('leaf', 'front')), may hold values from -0.125 to 0.125
- asm_owner: int32 [2, 16384, 1], P(None, ('leaf', 'front')), may hold values from 0 to 15; in each aligned block of 128 rows (0 to 127, 128 to 255, ..., all dimensions but the last counted through in order) at most 32 rows name the same one
- asm_row: int32 [2, 16384], P(None, ('leaf', 'front')), may hold values from 0 to 127
Outputs:
- solutions: float32 [3, 16384, 256], P(None, ('leaf', 'front'))
The draws below stay inside these ranges and needn't reach their ends.
Inputs may be any that keep to these rules, and one draw needn't show every extreme that they name: `asm_owner`: among the 128 update rows of one device at one level (aligned blocks of rows), at most 32 name the same owner, and some block reaches 32.
All inputs are finite; a program needn't handle non-finite values.
Results may differ from the reference program's by a relative error of at most 0.03.
Values may be sent and summed in bfloat16 or wider, within the bound.
A program may use at most 64 MiB of HBM per device.

```python
import math
import jax
import jax.numpy as jnp
import numpy as np
from jax import lax

PIV_DEV = 128
RHS = 256
LEVELS = 3
SPLIT = 8
BLOCK = 1024
ROWS = 16384
CAP = 32


def touch_ends(values, rng, least, top_value):
    index_at = [jax.random.randint(jax.random.fold_in(rng, axis), (), 0, length) for axis, length in enumerate(values.shape)]
    longest = values.shape.index(max(values.shape))
    neighbour = index_at[:longest] + [(index_at[longest] + 1) % values.shape[longest]] + index_at[longest + 1:]
    return values.at[tuple(index_at)].set(least).at[tuple(neighbour)].set(top_value)


def block_levels(stream_key, dims, shards, least, high):
    def one(dim, blocks):
        steps = jax.random.uniform(jax.random.fold_in(jax.random.fold_in(stream_key, 6), dim), (blocks,), jnp.float32, least / len(shards), high / len(shards))
        return jnp.repeat(jnp.exp(steps), dims[dim] // blocks).reshape((-1,) + (1,) * (len(dims) - dim - 1))

    level = one(*shards[0])
    for cut in shards[1:]:
        level = level * one(*cut)
    return level


def shared_out(own_key, own, number, rows, number_of, top, most, skew):
    sequence = jax.random.permutation(own_key, number_of)
    crowded, ordinary = shares(number_of, rows * top, most, skew, True), shares(number_of, rows * top, most, skew, False)
    places = jnp.arange(number_of)

    def named(sizes, rotation):
        used = int((sizes > 0).sum())
        fixed = max(1, used // 4)
        moved = fixed + (places - fixed + rotation * (used - fixed)) % max(1, number_of - fixed)
        return jnp.zeros((number_of,), jnp.int32).at[sequence[jnp.where(places < fixed, places, moved)]].set(jnp.asarray(sizes, jnp.int32))

    sizes = jnp.where(number % 4 == 0, named(crowded, number // 4), named(ordinary, number - number // 4 - 1))
    mixed = jax.random.permutation(jax.random.fold_in(own, 3), number_of)
    giver, taker = mixed[0:number_of // 2 * 2:2], mixed[1:number_of // 2 * 2:2]
    slack = jnp.minimum(sizes[giver] - 1, most - sizes[taker]) // 2
    slack = jnp.where((giver == sequence[0]) | (taker == sequence[0]) | (sizes[taker] == 0), 0, jnp.maximum(slack, 0))
    moved = jax.random.randint(jax.random.fold_in(own, 4), (number_of // 2,), 0, 1 << 20) % (slack + 1)
    sizes = sizes.at[giver].add(-moved).at[taker].add(moved)
    items = jnp.searchsorted(jnp.cumsum(sizes), jnp.arange(rows * top), side="right").astype(jnp.int32)
    table = items.reshape(top, rows).T
    table = table[jax.random.permutation(jax.random.fold_in(own, 1), rows)]
    rotation = jax.random.randint(jax.random.fold_in(own, 2), (rows, 1), 0, top)
    return jnp.take_along_axis(table, (jnp.arange(top)[None, :] + rotation) % top, axis=1)


def shares(amount, total, bound, slope, full):
    loads = [(1 << 20) // math.isqrt(grade ** slope) + 1 for grade in range(1, amount + 1)]
    largest = bound if full else min(bound, max(-(-total // amount), total * loads[0] // sum(loads)))
    least = 1 if total - largest >= amount - 1 else 0
    holding, rest = [largest] + [least] * (amount - 1), total - largest - least * (amount - 1)
    while rest > 0:
        candidates = [i for i in range(1, amount) if holding[i] < largest] or [i for i in range(1, amount) if holding[i] < bound]
        pool, budget = sum([loads[i] for i in candidates]), rest
        for i in candidates:
            more = min(bound - holding[i], max(1, budget * loads[i] // pool), rest)
            holding[i] = holding[i] + more
            rest = rest - more
    return np.array(holding)


def normal_values(rng, extent, spread, bound, cuts=(), kind=jnp.bfloat16):
    loudness = block_levels(rng, extent, cuts, -0.22, 0.18) if cuts else 1.0
    array = jax.random.normal(rng, extent, jnp.float32) * spread * loudness
    return jnp.minimum(jnp.maximum(array, -bound), bound).astype(kind)


def setup_inputs(seed: int = 0) -> dict:
    arg_keys = jax.random.split(jax.random.key(seed), 6)
    rhs = normal_values(arg_keys[0], (LEVELS, ROWS, RHS), 1.0, 6.0, ((1, 128),))
    inverse_blocks = normal_values(arg_keys[1], (ROWS, BLOCK * (2 ** LEVELS - 1)), (2 * BLOCK) ** -0.5, 0.125, ((0, 128),))
    update_blocks = normal_values(arg_keys[2], (ROWS, BLOCK * (2 ** (LEVELS - 1) - 1)), (2 * BLOCK) ** -0.5, 0.125, ((0, 128),))
    asm_owner_keys = jax.random.split(jax.random.fold_in(arg_keys[3], 1), (LEVELS - 1) * ROWS // PIV_DEV)
    asm_owner_turns = jax.random.permutation(jax.random.fold_in(arg_keys[3], 3), (LEVELS - 1) * ROWS // PIV_DEV)
    asm_owner = jax.vmap(lambda own, number: shared_out(jax.random.fold_in(arg_keys[3], 2), own, number, PIV_DEV, 2 * SPLIT, 1, CAP, 1))(asm_owner_keys, asm_owner_turns).reshape((LEVELS - 1, ROWS, 1))
    asm_row = touch_ends(jax.random.randint(arg_keys[4], (LEVELS - 1, ROWS), 0, PIV_DEV), jax.random.fold_in(arg_keys[4], 1), 0, PIV_DEV - 1).astype(jnp.int32)
    return {"rhs": rhs, "inverse_blocks": inverse_blocks, "update_blocks": update_blocks, "asm_owner": asm_owner, "asm_row": asm_row}


def apply_blocks(matrix, vectors, front_rows):
    front_total = vectors.shape[0] // front_rows
    stacked = (matrix.reshape(front_total, front_rows, front_rows), vectors.reshape(front_total, front_rows, vectors.shape[1]))
    result = lax.map(lambda paired: jnp.dot(paired[0], paired[1], preferred_element_type=jnp.float32), stacked)
    return result.reshape(vectors.shape[0], vectors.shape[1])


def apply_transposed(matrix, vectors, front_rows):
    front_total = vectors.shape[0] // front_rows
    stacked = (matrix.reshape(front_total, front_rows, front_rows), vectors.reshape(front_total, front_rows, vectors.shape[1]))
    result = lax.map(lambda paired: lax.dot_general(paired[0], paired[1], (((0,), (0,)), ((), ())), preferred_element_type=jnp.float32), stacked)
    return result.reshape(vectors.shape[0], vectors.shape[1])


def reference(rhs, inverse_blocks, update_blocks, asm_owner, asm_row):
    leaf_rows = SPLIT * PIV_DEV
    row_ids = jnp.arange(ROWS, dtype=jnp.int32)
    leaf_of = row_ids // leaf_rows
    targets = []
    for level_index in range(LEVELS - 1):
        owner_ids = asm_owner[level_index, :, 0]
        upper_side = owner_ids // SPLIT
        front_of = owner_ids % SPLIT
        pair_span = 2 ** level_index
        lower_leaf = leaf_of - (leaf_of // pair_span) % 2 * pair_span
        targets.append(((lower_leaf + upper_side * pair_span) * SPLIT + front_of) * PIV_DEV + asm_row[level_index])
    assembled = jnp.zeros((ROWS, RHS), jnp.float32)
    solved_all = []
    for level_index in range(LEVELS):
        front_rows = leaf_rows * 2 ** level_index
        column_start = leaf_rows * (2 ** level_index - 1)
        pivots = (rhs[level_index].astype(jnp.float32) - assembled).astype(jnp.bfloat16)
        solved = apply_blocks(inverse_blocks[:, column_start:column_start + front_rows], pivots, front_rows).astype(jnp.bfloat16)
        solved_all.append(solved)
        if level_index + 1 < LEVELS:
            update = apply_blocks(update_blocks[:, column_start:column_start + front_rows], solved, front_rows).astype(jnp.bfloat16)
            assembled = jnp.zeros((ROWS, RHS), jnp.float32).at[targets[level_index]].add(update.astype(jnp.float32))
    solutions = [None] * LEVELS
    below = None
    for level_index in reversed(range(LEVELS)):
        front_rows = leaf_rows * 2 ** level_index
        column_start = leaf_rows * (2 ** level_index - 1)
        if level_index + 1 == LEVELS:
            weights = solved_all[level_index]
        else:
            fetched = below[targets[level_index]]
            carried = apply_transposed(update_blocks[:, column_start:column_start + front_rows], fetched, front_rows)
            weights = (solved_all[level_index].astype(jnp.float32) - carried).astype(jnp.bfloat16)
        solution = apply_transposed(inverse_blocks[:, column_start:column_start + front_rows], weights, front_rows)
        solutions[level_index] = solution
        below = solution.astype(jnp.bfloat16)
    return jnp.stack(solutions)
```

```python
import functools

import jax
import jax.numpy as jnp
from jax import lax
from jax.experimental import pallas as pl
from jax.experimental.pallas import tpu as pltpu
from jax.sharding import PartitionSpec as P

MESH = pl.DeviceIdType.MESH
F32, BF16 = jnp.float32, jnp.bfloat16

CHAINS = 2
ROW = 128
UNIT = 256
HALF = 128
NX, NZ = 4, 4
LEAF = UNIT * NZ
WIDTH = HALF // CHAINS
D_AT = (0, LEAF, 3 * LEAF)
E_AT = (0, LEAF)

Z_PEERS = (2, 1, 3)
PAIR_PEERS = ((1, 2), (1, 1), (1, 3), (0, 2), (1, 0), (0, 1), (0, 3))
QUAD_PEERS = tuple((dx, dz) for dx in (2, 1, 3, 0) for dz in (2, 1, 3, 0) if dx or dz)

CHAINED = (
    ("a0", 3), ("a1", 3), ("u0", 7), ("s1", 7), ("u1", 15), ("f1", 15), ("e1", 7), ("f0", 7), ("w0", 3), ("l0", 3),
    ("d2x", 3), ("d2z", 3), ("d1x", 1), ("d1z", 3),
)
SINGLE = (("core", 9), ("tz", 3), ("tx", 3), ("r1z", 3), ("r1x", 1), ("r2z", 3), ("r2x", 3), ("out", 3))
SEM_AT, SEM_COUNT = {}, 0
for _name, _n in CHAINED:
    SEM_AT[_name] = SEM_COUNT
    SEM_COUNT += _n * CHAINS
for _name, _n in SINGLE:
    SEM_AT[_name] = SEM_COUNT
    SEM_COUNT += _n


def nt(left, right):
    return lax.dot_general(left, right, (((1,), (1,)), ((), ())), preferred_element_type=F32)


def nn(left, right):
    return lax.dot_general(left, right, (((1,), (0,)), ((), ())), preferred_element_type=F32)


def kernel(
    owner_ref, row_ref, rhs_hbm, d_hbm, e_hbm, out_hbm,
    rhs_v, dm, em, m1, m2, swap, rt, tg, zr1, zr2, select,
    s0b, u0b, s1b, u1b, s2b, w1b,
    a0r, a1r, u0r, s1r, u1r, y1, y2,
    f1s, f1r, e1s, e1r, f0s, f0r, w0s, w0r, l0s, l0r,
    d2xs, d2xr, d2zs, d2zr, d1xs, d1xr, d1zs, d1zr,
    sol, stage_own, stage_other,
    ssem, rsem, lsem,
):
    leaf, front = lax.axis_index("leaf"), lax.axis_index("front")
    x, y = lax.rem(leaf, NX), leaf // NX
    z, c = front // 2, lax.rem(front, 2)
    other = 1 - c
    xp = x + 1 - 2 * lax.rem(x, 2)
    xpar = lax.rem(x, 2)

    def dev(xx, zz):
        return (y * NX + xx, zz * 2 + c)

    core = (leaf, z * 2 + other)

    def zp(d):
        return lax.rem(z + d, NZ)

    def zm(d):
        return lax.rem(z + NZ - d, NZ)

    def xq(d):
        return lax.rem(x + d, NX)

    def xm(d):
        return lax.rem(x + NX - d, NX)

    def at(value):
        return pl.multiple_of(value, UNIT)

    def copy(src, dst, sem, device):
        return pltpu.make_async_remote_copy(
            src_ref=src, dst_ref=dst, send_sem=ssem.at[sem], recv_sem=rsem.at[sem], device_id=device, device_id_type=MESH
        )

    def chains(body):
        def step(ch, carry):
            body(ch)
            return carry

        lax.fori_loop(0, CHAINS, step, 0)

    def cols(ch):
        return pl.ds(pl.multiple_of(ch * WIDTH, WIDTH), WIDTH)

    def gather_z(name, src, dst, ch):
        return [copy(src.at[ch], dst.at[ch, i], SEM_AT[name] + ch * 3 + i, dev(x, zp(d))) for i, d in enumerate(Z_PEERS)]

    def gather_pair(name, src, dst, ch):
        return [
            copy(src.at[ch], dst.at[ch, i], SEM_AT[name] + ch * 7 + i, dev(xp if px else x, zp(d)))
            for i, (px, d) in enumerate(PAIR_PEERS)
        ]

    def gather_quad(name, src, dst, ch):
        return [
            copy(src.at[ch], dst.at[ch, i], SEM_AT[name] + ch * 15 + i, dev(xq(dx), zp(d)))
            for i, (dx, d) in enumerate(QUAD_PEERS)
        ]

    def reduce_z(name, src, dst, ch):
        return [
            copy(src.at[ch, zp(d)], dst.at[ch, i], SEM_AT[name] + ch * 3 + i, dev(x, zp(d))) for i, d in enumerate(Z_PEERS)
        ]

    def reduce_pair(name, src, dst, ch):
        out = []
        for i, (px, d) in enumerate(PAIR_PEERS):
            xx = xp if px else x
            out.append(copy(src.at[ch, lax.rem(xx, 2), zp(d)], dst.at[ch, i], SEM_AT[name] + ch * 7 + i, dev(xx, zp(d))))
        return out

    def reduce_quad(name, src, dst, ch):
        return [
            copy(src.at[ch, xq(dx), zp(d)], dst.at[ch, i], SEM_AT[name] + ch * 15 + i, dev(xq(dx), zp(d)))
            for i, (dx, d) in enumerate(QUAD_PEERS)
        ]

    def x_quad(name, src, dst, ch):
        return [copy(src.at[ch, xq(d)], dst.at[ch, i], SEM_AT[name] + ch * 3 + i, dev(xq(d), z)) for i, d in enumerate(Z_PEERS)]

    def x_pair(name, src, dst, ch):
        return [copy(src.at[ch, 1 - xpar], dst.at[ch, 0], SEM_AT[name] + ch, dev(xp, z))]

    def start(copies):
        for one in copies:
            one.start()

    def received(copies):
        for one in copies:
            one.wait_recv()

    def sent(copies):
        for one in copies:
            one.wait_send()

    mine, theirs = pl.ds(pl.multiple_of(c * ROW, ROW), ROW), pl.ds(pl.multiple_of(other * ROW, ROW), ROW)
    spans = ((d_hbm, dm, 0, LEAF), (e_hbm, em, 0, LEAF), (d_hbm, dm, LEAF, 2 * LEAF), (e_hbm, em, LEAF, 2 * LEAF), (d_hbm, dm, 3 * LEAF, 4 * LEAF))

    load_rhs = pltpu.make_async_copy(rhs_hbm, rhs_v, lsem.at[0])
    load_rhs.start()
    loads = [
        pltpu.make_async_copy(src.at[:, pl.ds(a, n)], dst.at[mine, pl.ds(a, n)], lsem.at[1 + i])
        for i, (src, dst, a, n) in enumerate(spans)
    ]
    for one in loads:
        one.start()
    barrier = pltpu.get_barrier_semaphore()
    pl.semaphore_signal(barrier, inc=1, device_id=core, device_id_type=MESH)
    for dx, d in QUAD_PEERS:
        pl.semaphore_signal(barrier, inc=1, device_id=dev(xq(dx), zp(d)), device_id_type=MESH)

    eye = lax.broadcasted_iota(jnp.int32, (ROW, ROW), 0) == lax.broadcasted_iota(jnp.int32, (ROW, ROW), 1)
    for level in range(2):
        owner = jnp.sum(jnp.where(eye, owner_ref[level].astype(F32), 0.0), axis=0, keepdims=True).astype(jnp.int32)
        row = row_ref[level : level + 1, :]
        if level == 0:
            target = owner * ROW + row
        else:
            target = xpar * LEAF + (owner // 8) * (2 * LEAF) + lax.rem(owner, 8) * ROW + row
        tg[0, 0, level : level + 1, mine] = target

    load_rhs.wait()
    for level in range(3):
        rt[level, :, mine] = rhs_v[level, :, mine].astype(F32).T.astype(BF16)
        swap[level] = rhs_v[level, :, theirs].astype(F32).T.astype(BF16)

    pl.semaphore_wait(barrier, 16)
    swaps = [copy(swap.at[level], rt.at[level, :, mine], SEM_AT["core"] + level, core) for level in range(3)]
    swaps.append(copy(tg.at[0, 0, :, mine], tg.at[0, 0, :, mine], SEM_AT["core"] + 3, core))
    swaps += [
        copy(src.at[:, pl.ds(a, n)], dst.at[mine, pl.ds(a, n)], SEM_AT["core"] + 4 + i, core)
        for i, (src, dst, a, n) in enumerate(spans)
    ]
    start(swaps)

    def gather_r0(ch):
        return [
            copy(rt.at[0, cols(ch)], a0r.at[ch, i], SEM_AT["a0"] + ch * 3 + i, dev(x, zp(d))) for i, d in enumerate(Z_PEERS)
        ]

    swaps[0].wait_recv()
    chains(lambda ch: start(gather_r0(ch)))
    t_z = [copy(tg.at[0, 0], tg.at[0, d], SEM_AT["tz"] + i, dev(x, zp(d))) for i, d in enumerate(Z_PEERS)]
    t_x = [copy(tg.at[0], tg.at[d], SEM_AT["tx"] + i, dev(xq(d), z)) for i, d in enumerate(Z_PEERS)]
    r1_z = [copy(rt.at[1], zr1.at[0, d], SEM_AT["r1z"] + i, dev(x, zp(d))) for i, d in enumerate(Z_PEERS)]
    r2_z = [copy(rt.at[2], zr2.at[0, d], SEM_AT["r2z"] + i, dev(x, zp(d))) for i, d in enumerate(Z_PEERS)]
    r1_x = [copy(zr1.at[0], zr1.at[1], SEM_AT["r1x"], dev(xp, z))]
    r2_x = [copy(zr2.at[0], zr2.at[d], SEM_AT["r2x"] + i, dev(xq(d), z)) for i, d in enumerate(Z_PEERS)]
    swaps[3].wait_recv()
    start(t_z)
    swaps[1].wait_recv()
    start(r1_z)
    swaps[2].wait_recv()
    start(r2_z)
    zr1[0, 0] = rt[1]
    zr2[0, 0] = rt[2]

    def d_block(level, index):
        return dm[:, pl.ds(at(D_AT[level] + index * UNIT), UNIT)]

    def e_block(level, index):
        return em[:, pl.ds(at(E_AT[level] + index * UNIT), UNIT)]

    def pair_index(px, d):
        return lax.rem(xp if px else x, 2) * NZ + zm(d)

    loads[0].wait()
    swaps[4].wait_recv()

    def solve0(ch):
        total = nt(rt[0, cols(ch), :], d_block(0, z))
        for i, d in enumerate(Z_PEERS):
            gather_r0(ch)[i].wait_recv()
            total += nt(a0r[ch, i], d_block(0, zm(d)))
        s0b[ch] = total.astype(BF16)
        start(gather_z("a1", s0b, a1r, ch))

    chains(solve0)

    received(t_z)
    start(t_x)
    received(r1_z)
    start(r1_x)
    received(r2_z)
    start(r2_x)

    loads[1].wait()
    swaps[5].wait_recv()

    def update0(ch):
        total = nt(s0b[ch], e_block(0, z))
        copies = gather_z("a1", s0b, a1r, ch)
        for i, d in enumerate(Z_PEERS):
            copies[i].wait_recv()
            total += nt(a1r[ch, i], e_block(0, zm(d)))
        u0b[ch] = total.astype(BF16)
        start(gather_pair("u0", u0b, u0r, ch))

    chains(update0)

    def fill_select(target, base, count):
        for k in range(count):
            rows = lax.broadcasted_iota(jnp.int32, (UNIT, UNIT), 0) + (base + k * UNIT)
            select[k * UNIT : (k + 1) * UNIT, :] = jnp.where(rows == target, 1.0, 0.0).astype(BF16)

    loads[2].wait()
    swaps[6].wait_recv()
    received(t_x)

    def select1(j, carry):
        px, d = j // NZ, lax.rem(j, NZ)
        dx = px * (3 - 2 * xpar)
        source = lax.rem(x + px, 2) * NZ + zm(d)
        target = tg[dx, d, 0:1, :]
        total = jnp.zeros((UNIT, UNIT), F32)
        for part in range(2):
            fill_select(target, part * LEAF, 4)
            total += nn(dm[:, D_AT[1] + part * LEAF : D_AT[1] + (part + 1) * LEAF], select[...])
        m1[:, pl.ds(at(source * UNIT), UNIT)] = total.astype(BF16)
        return carry

    lax.fori_loop(0, 2 * NZ, select1, 0)
    received(r1_x)

    def rhs1(ch):
        total = jnp.zeros((WIDTH, UNIT), F32)
        for px in range(2):
            for d in range(NZ):
                total += nt(zr1[px, d, cols(ch), :], d_block(1, pair_index(px, d)))
        y1[ch] = total

    chains(rhs1)

    def solve1(ch):
        total = nt(u0b[ch], m1[:, pl.ds(at((xpar * NZ + z) * UNIT), UNIT)])
        copies = gather_pair("u0", u0b, u0r, ch)
        for i, (px, d) in reversed(list(enumerate(PAIR_PEERS))):
            copies[i].wait_recv()
            total += nt(u0r[ch, i], m1[:, pl.ds(at(pair_index(px, d) * UNIT), UNIT)])
        s1b[ch] = (y1[ch] - total).astype(BF16)
        start(gather_pair("s1", s1b, s1r, ch))

    chains(solve1)

    loads[4].wait()
    swaps[8].wait_recv()

    def select2(j, carry):
        dx, d = j // NZ, lax.rem(j, NZ)
        xj = xm(dx)
        target = tg[dx, d, 1:2, :]
        total = jnp.zeros((UNIT, UNIT), F32)
        for side in range(2):
            base = lax.rem(xj, 2) * LEAF + side * 2 * LEAF
            fill_select(target, base, 4)
            total += nn(dm[:, pl.ds(at(D_AT[2] + base), LEAF)], select[...])
        m2[:, pl.ds(at((xj * NZ + zm(d)) * UNIT), UNIT)] = total.astype(BF16)
        return carry

    lax.fori_loop(0, 8, select2, 0)

    loads[3].wait()
    swaps[7].wait_recv()

    def update1(ch):
        total = nt(s1b[ch], e_block(1, xpar * NZ + z))
        copies = gather_pair("s1", s1b, s1r, ch)
        for i, (px, d) in reversed(list(enumerate(PAIR_PEERS))):
            copies[i].wait_recv()
            total += nt(s1r[ch, i], e_block(1, pair_index(px, d)))
        u1b[ch] = total.astype(BF16)
        start(gather_quad("u1", u1b, u1r, ch))

    chains(update1)

    lax.fori_loop(8, 16, select2, 0)
    received(r2_x)

    def rhs2(ch):
        total = jnp.zeros((WIDTH, UNIT), F32)
        for dx in range(NX):
            for d in range(NZ):
                total += nt(zr2[dx, d, cols(ch), :], d_block(2, xm(dx) * NZ + zm(d)))
        y2[ch] = total

    chains(rhs2)

    def spread(matrix, base, vector, dst, ch, leaves):
        for k in range(leaves):
            part = nn(vector, matrix[:, base + k * LEAF : base + (k + 1) * LEAF]).astype(BF16)
            for i in range(NZ):
                if leaves == 1:
                    dst[ch, i] = part[:, i * UNIT : (i + 1) * UNIT]
                else:
                    dst[ch, k, i] = part[:, i * UNIT : (i + 1) * UNIT]

    def solve2(ch):
        total = nt(u1b[ch], m2[:, pl.ds(at((x * NZ + z) * UNIT), UNIT)])
        copies = gather_quad("u1", u1b, u1r, ch)
        for i, (dx, d) in reversed(list(enumerate(QUAD_PEERS))):
            copies[i].wait_recv()
            total += nt(u1r[ch, i], m2[:, pl.ds(at((xm(dx) * NZ + zm(d)) * UNIT), UNIT)])
        solved = (y2[ch] - total).astype(BF16)
        s2b[ch] = solved
        spread(m2, 0, solved, f1s, ch, 4)
        start(reduce_quad("f1", f1s, f1r, ch))

    chains(solve2)

    def back2(ch):
        spread(dm, D_AT[2], s2b[ch], d2xs, ch, 4)
        start(x_quad("d2x", d2xs, d2xr, ch))

    chains(back2)

    def summed(copies, own, dst, ch):
        total = own.astype(F32)
        for i in reversed(range(len(copies))):
            copies[i].wait_recv()
            total += dst[ch, i].astype(F32)
        return total

    def fetch1(ch):
        fetched = summed(reduce_quad("f1", f1s, f1r, ch), f1s[ch, x, z], f1r, ch).astype(BF16)
        spread(em, E_AT[1], fetched, e1s, ch, 2)
        start(reduce_pair("e1", e1s, e1r, ch))

    chains(fetch1)

    def weigh1(ch):
        carried = summed(reduce_pair("e1", e1s, e1r, ch), e1s[ch, xpar, z], e1r, ch)
        weights = (s1b[ch].astype(F32) - carried).astype(BF16)
        w1b[ch] = weights
        spread(m1, 0, weights, f0s, ch, 2)
        start(reduce_pair("f0", f0s, f0r, ch))

    chains(weigh1)

    def back2z(ch):
        received(x_quad("d2x", d2xs, d2xr, ch))
        for k in range(NZ):
            total = d2xs[ch, x, k].astype(F32)
            for i in range(3):
                total += d2xr[ch, i, k].astype(F32)
            d2zs[ch, k] = total.astype(BF16)
        start(reduce_z("d2z", d2zs, d2zr, ch))

    chains(back2z)

    def back1(ch):
        spread(dm, D_AT[1], w1b[ch], d1xs, ch, 2)
        start(x_pair("d1x", d1xs, d1xr, ch))

    chains(back1)

    def fetch0(ch):
        fetched = summed(reduce_pair("f0", f0s, f0r, ch), f0s[ch, xpar, z], f0r, ch).astype(BF16)
        spread(em, E_AT[0], fetched, w0s, ch, 1)
        start(reduce_z("w0", w0s, w0r, ch))

    chains(fetch0)

    def back1z(ch):
        received(x_pair("d1x", d1xs, d1xr, ch))
        for k in range(NZ):
            d1zs[ch, k] = (d1xs[ch, xpar, k].astype(F32) + d1xr[ch, 0, k].astype(F32)).astype(BF16)
        start(reduce_z("d1z", d1zs, d1zr, ch))

    chains(back1z)

    def weigh0(ch):
        carried = summed(reduce_z("w0", w0s, w0r, ch), w0s[ch, z], w0r, ch)
        weights = (s0b[ch].astype(F32) - carried).astype(BF16)
        spread(dm, D_AT[0], weights, l0s, ch, 1)
        start(reduce_z("l0", l0s, l0r, ch))

    chains(weigh0)

    def out_copies(level):
        keep = pltpu.make_async_copy(stage_own.at[level], out_hbm.at[level, :, mine], lsem.at[6 + level])
        hand = copy(stage_other.at[level], out_hbm.at[level, :, mine], SEM_AT["out"] + level, core)
        return keep, hand

    def finish(level, name, src, dst):
        def one(ch):
            sol[level, cols(ch), :] = summed(reduce_z(name, src, dst, ch), src[ch, z], dst, ch)

        chains(one)
        stage_other[level] = sol[level, :, theirs].T
        keep, hand = out_copies(level)
        hand.start()
        stage_own[level] = sol[level, :, mine].T
        keep.start()

    finish(2, "d2z", d2zs, d2zr)
    finish(1, "d1z", d1zs, d1zr)

    sent(swaps + t_z + t_x + r1_z + r1_x + r2_z + r2_x)

    def all_sent(ch):
        sent(gather_r0(ch))
        sent(gather_z("a1", s0b, a1r, ch))
        sent(gather_pair("u0", u0b, u0r, ch))
        sent(gather_pair("s1", s1b, s1r, ch))
        sent(gather_quad("u1", u1b, u1r, ch))
        sent(reduce_quad("f1", f1s, f1r, ch))
        sent(x_quad("d2x", d2xs, d2xr, ch))
        sent(reduce_z("d2z", d2zs, d2zr, ch))
        sent(reduce_pair("e1", e1s, e1r, ch))
        sent(reduce_pair("f0", f0s, f0r, ch))
        sent(x_pair("d1x", d1xs, d1xr, ch))
        sent(reduce_z("d1z", d1zs, d1zr, ch))
        sent(reduce_z("w0", w0s, w0r, ch))

    chains(all_sent)

    finish(0, "l0", l0s, l0r)
    chains(lambda ch: sent(reduce_z("l0", l0s, l0r, ch)))
    for level in range(3):
        keep, hand = out_copies(level)
        keep.wait()
        hand.wait()


def shards(rhs, inverse_blocks, update_blocks, asm_owner, asm_row):
    k, w = CHAINS, WIDTH
    vmem = pl.BlockSpec(memory_space=pltpu.VMEM)
    hbm = pl.BlockSpec(memory_space=pl.ANY)
    block = lambda *lead: pltpu.VMEM((k, *lead, w, UNIT), BF16)
    return pl.pallas_call(
        kernel,
        out_shape=jax.ShapeDtypeStruct(rhs.shape, F32),
        in_specs=[vmem, vmem, hbm, hbm, hbm],
        out_specs=hbm,
        scratch_shapes=[
            pltpu.VMEM((3, ROW, 2 * HALF), BF16),
            pltpu.VMEM((UNIT, 7 * LEAF), BF16),
            pltpu.VMEM((UNIT, 3 * LEAF), BF16),
            pltpu.VMEM((UNIT, 2 * LEAF), BF16),
            pltpu.VMEM((UNIT, 4 * LEAF), BF16),
            pltpu.VMEM((3, HALF, ROW), BF16),
            pltpu.VMEM((3, HALF, UNIT), BF16),
            pltpu.VMEM((NX, NZ, 8, UNIT), jnp.int32),
            pltpu.VMEM((2, NZ, HALF, UNIT), BF16),
            pltpu.VMEM((NX, NZ, HALF, UNIT), BF16),
            pltpu.VMEM((LEAF, UNIT), BF16),
            block(), block(), block(), block(), block(), block(),
            block(3), block(3), block(7), block(7), block(15),
            pltpu.VMEM((k, w, UNIT), F32),
            pltpu.VMEM((k, w, UNIT), F32),
            block(4, 4), block(15), block(2, 4), block(7), block(2, 4), block(7),
            block(4), block(3), block(4), block(3),
            block(4, 4), block(3, 4), block(4), block(3),
            block(2, 4), block(1, 4), block(4), block(3),
            pltpu.VMEM((3, HALF, UNIT), F32),
            pltpu.VMEM((3, ROW, HALF), F32),
            pltpu.VMEM((3, ROW, HALF), F32),
            pltpu.SemaphoreType.DMA((SEM_COUNT,)),
            pltpu.SemaphoreType.DMA((SEM_COUNT,)),
            pltpu.SemaphoreType.DMA((9,)),
        ],
        compiler_params=pltpu.CompilerParams(collective_id=0, has_side_effects=True, vmem_limit_bytes=56 * 2**20),
    )(asm_owner, asm_row, rhs, inverse_blocks, update_blocks)


def solution(mesh):
    placed = (
        P(None, ("leaf", "front"), None),
        P(("leaf", "front"), None),
        P(("leaf", "front"), None),
        P(None, ("leaf", "front"), None),
        P(None, ("leaf", "front")),
    )
    return jax.shard_map(
        shards, mesh=mesh, in_specs=placed, out_specs=P(None, ("leaf", "front"), None), check_vma=False
    )
```

```python
import functools

import jax
import jax.numpy as jnp
from jax import lax
from jax.experimental import pallas as pl
from jax.experimental.pallas import tpu as pltpu
from jax.sharding import PartitionSpec as P

MESH = pl.DeviceIdType.MESH
F32, BF16 = jnp.float32, jnp.bfloat16

CHAINS = 2
ROW = 128
UNIT = 256
HALF = 128
NX, NZ = 4, 4
LEAF = UNIT * NZ
WIDTH = HALF // CHAINS
D_AT = (0, LEAF)
E_AT = (0, LEAF)

Z_PEERS = (2, 1, 3)
PAIR_PEERS = ((1, 2), (1, 1), (1, 3), (0, 2), (1, 0), (0, 1), (0, 3))
X_PEERS = (2, 1, 3)
QUAD_PEERS = tuple((dx, dz) for dx in (2, 1, 3, 0) for dz in (2, 1, 3, 0) if dx or dz)

CHAINED = (
    ("a0", 3), ("a1", 3), ("u0", 7), ("s1", 7), ("u1", 7), ("s2r", 3), ("s2a", 3), ("f1", 7), ("e1", 7), ("f0", 7),
    ("w0", 3), ("l0", 3), ("d2z", 3), ("d1x", 1), ("d1z", 3),
)
SINGLE = (("core", 9), ("block", 3), ("hand", 3), ("tz", 3), ("tx", 3), ("r1z", 3), ("r1x", 1), ("r2z", 3), ("out", 3))
SEM_AT, SEM_COUNT = {}, 0
for _name, _n in CHAINED:
    SEM_AT[_name] = SEM_COUNT
    SEM_COUNT += _n * CHAINS
for _name, _n in SINGLE:
    SEM_AT[_name] = SEM_COUNT
    SEM_COUNT += _n


def nt(left, right):
    return lax.dot_general(left, right, (((1,), (1,)), ((), ())), preferred_element_type=F32)


def nn(left, right):
    return lax.dot_general(left, right, (((1,), (0,)), ((), ())), preferred_element_type=F32)


def kernel(
    owner_ref, row_ref, rhs_hbm, d_hbm, e_hbm, out_hbm,
    rhs_v, dm, d2, em, m1, m2, swap, rt, tg, zr1, zr2, select,
    s0b, u0b, s1b, u1b, s2b, w1b,
    a0r, a1r, u0r, s1r, u1r, y1, y2, s2rs, s2rr, s2ar,
    f1s, f1r, e1s, e1r, f0s, f0r, w0s, w0r, l0s, l0r,
    d2zs, d2zr, d1xs, d1xr, d1zs, d1zr,
    sol, stage_own, stage_other,
    ssem, rsem, lsem,
):
    leaf, front = lax.axis_index("leaf"), lax.axis_index("front")
    x, y = lax.rem(leaf, NX), leaf // NX
    z, c = front // 2, lax.rem(front, 2)
    other = 1 - c
    xp = x + 1 - 2 * lax.rem(x, 2)
    xpar = lax.rem(x, 2)
    xo = lax.rem(x + 2, NX)

    def dev(xx, zz):
        return (y * NX + xx, zz * 2 + c)

    core = (leaf, z * 2 + other)

    def zp(d):
        return lax.rem(z + d, NZ)

    def zm(d):
        return lax.rem(z + NZ - d, NZ)

    def xq(d):
        return lax.rem(x + d, NX)

    def xm(d):
        return lax.rem(x + NX - d, NX)

    def at(value):
        return pl.multiple_of(value, UNIT)

    def copy(src, dst, sem, device):
        return pltpu.make_async_remote_copy(
            src_ref=src, dst_ref=dst, send_sem=ssem.at[sem], recv_sem=rsem.at[sem], device_id=device, device_id_type=MESH
        )

    def chains(body):
        def step(ch, carry):
            body(ch)
            return carry

        lax.fori_loop(0, CHAINS, step, 0)

    def cols(ch):
        return pl.ds(pl.multiple_of(ch * WIDTH, WIDTH), WIDTH)

    def gather_z(name, src, dst, ch):
        return [copy(src.at[ch], dst.at[ch, i], SEM_AT[name] + ch * 3 + i, dev(x, zp(d))) for i, d in enumerate(Z_PEERS)]

    def gather_pair(name, src, dst, ch):
        return [
            copy(src.at[ch], dst.at[ch, i], SEM_AT[name] + ch * 7 + i, dev(xp if px else x, zp(d)))
            for i, (px, d) in enumerate(PAIR_PEERS)
        ]

    def gather_skip(name, src, dst, ch):
        return [
            copy(src.at[ch], dst.at[ch, i], SEM_AT[name] + ch * 7 + i, dev(xo if px else x, zp(d)))
            for i, (px, d) in enumerate(PAIR_PEERS)
        ]

    def gather_x(name, src, dst, ch):
        return [copy(src.at[ch], dst.at[ch, i], SEM_AT[name] + ch * 3 + i, dev(xq(d), z)) for i, d in enumerate(X_PEERS)]

    def reduce_z(name, src, dst, ch):
        return [
            copy(src.at[ch, zp(d)], dst.at[ch, i], SEM_AT[name] + ch * 3 + i, dev(x, zp(d))) for i, d in enumerate(Z_PEERS)
        ]

    def reduce_pair(name, src, dst, ch):
        out = []
        for i, (px, d) in enumerate(PAIR_PEERS):
            xx = xp if px else x
            out.append(copy(src.at[ch, lax.rem(xx, 2), zp(d)], dst.at[ch, i], SEM_AT[name] + ch * 7 + i, dev(xx, zp(d))))
        return out

    def reduce_skip(name, src, dst, ch):
        out = []
        for i, (px, d) in enumerate(PAIR_PEERS):
            xx = xo if px else x
            out.append(copy(src.at[ch, xx // 2, zp(d)], dst.at[ch, i], SEM_AT[name] + ch * 7 + i, dev(xx, zp(d))))
        return out

    def reduce_x(name, src, dst, ch):
        return [copy(src.at[ch, xq(d)], dst.at[ch, i], SEM_AT[name] + ch * 3 + i, dev(xq(d), z)) for i, d in enumerate(X_PEERS)]

    def x_pair(name, src, dst, ch):
        return [copy(src.at[ch, 1 - xpar], dst.at[ch, 0], SEM_AT[name] + ch, dev(xp, z))]

    def start(copies):
        for one in copies:
            one.start()

    def received(copies):
        for one in copies:
            one.wait_recv()

    def sent(copies):
        for one in copies:
            one.wait_send()

    mine, theirs = pl.ds(pl.multiple_of(c * ROW, ROW), ROW), pl.ds(pl.multiple_of(other * ROW, ROW), ROW)
    spans = ((d_hbm, dm, 0, LEAF), (e_hbm, em, 0, LEAF), (d_hbm, dm, LEAF, 2 * LEAF), (e_hbm, em, LEAF, 2 * LEAF))

    def d2_columns(leaf_x):
        return d_hbm.at[:, pl.ds(pl.multiple_of((3 + leaf_x) * LEAF, LEAF), LEAF)]

    def d2_rows(leaf_x):
        return d2.at[pl.ds(pl.multiple_of(leaf_x * UNIT + c * ROW, ROW), ROW)]

    load_rhs = pltpu.make_async_copy(rhs_hbm, rhs_v, lsem.at[0])
    load_rhs.start()
    loads = [
        pltpu.make_async_copy(src.at[:, pl.ds(a, n)], dst.at[mine, pl.ds(a, n)], lsem.at[1 + i])
        for i, (src, dst, a, n) in enumerate(spans)
    ]
    loads.append(pltpu.make_async_copy(d2_columns(x), d2_rows(x), lsem.at[5]))
    for one in loads:
        one.start()
    barrier = pltpu.get_barrier_semaphore()
    pl.semaphore_signal(barrier, inc=1, device_id=core, device_id_type=MESH)
    for dx, d in QUAD_PEERS:
        pl.semaphore_signal(barrier, inc=1, device_id=dev(xq(dx), zp(d)), device_id_type=MESH)

    for level in range(2):
        owner = owner_ref[level]
        row = row_ref[level : level + 1, :]
        if level == 0:
            target = owner * ROW + row
        else:
            target = xpar * LEAF + (owner // 8) * (2 * LEAF) + lax.rem(owner, 8) * ROW + row
        tg[0, 0, level : level + 1, mine] = target

    load_rhs.wait()
    for level in range(3):
        rt[level, :, mine] = rhs_v[level, :, mine].astype(F32).T.astype(BF16)
        swap[level] = rhs_v[level, :, theirs].astype(F32).T.astype(BF16)

    pl.semaphore_wait(barrier, 16)
    swaps = [copy(swap.at[level], rt.at[level, :, mine], SEM_AT["core"] + level, core) for level in range(3)]
    swaps.append(copy(tg.at[0, 0, :, mine], tg.at[0, 0, :, mine], SEM_AT["core"] + 3, core))
    swaps += [
        copy(src.at[:, pl.ds(a, n)], dst.at[mine, pl.ds(a, n)], SEM_AT["core"] + 4 + i, core)
        for i, (src, dst, a, n) in enumerate(spans)
    ]
    swaps.append(copy(d2_columns(x), d2_rows(x), SEM_AT["core"] + 8, core))
    start(swaps)

    def gather_r0(ch):
        return [
            copy(rt.at[0, cols(ch)], a0r.at[ch, i], SEM_AT["a0"] + ch * 3 + i, dev(x, zp(d))) for i, d in enumerate(Z_PEERS)
        ]

    swaps[0].wait_recv()
    chains(lambda ch: start(gather_r0(ch)))
    t_z = [copy(tg.at[0, 0], tg.at[0, d], SEM_AT["tz"] + i, dev(x, zp(d))) for i, d in enumerate(Z_PEERS)]
    t_x = [copy(tg.at[0], tg.at[d], SEM_AT["tx"] + i, dev(xq(d), z)) for i, d in enumerate(Z_PEERS)]
    r1_x = [copy(rt.at[1], zr1.at[1, 0], SEM_AT["r1x"], dev(xp, z))]
    r1_z = [copy(zr1.at[:, 0], zr1.at[:, d], SEM_AT["r1z"] + i, dev(x, zp(d))) for i, d in enumerate(Z_PEERS)]
    r2_z = [copy(rt.at[2], zr2.at[d], SEM_AT["r2z"] + i, dev(x, zp(d))) for i, d in enumerate(Z_PEERS)]
    blocks = [copy(d2_columns(xq(d)), d2_rows(x), SEM_AT["block"] + i, dev(xq(d), z)) for i, d in enumerate(X_PEERS)]
    hands = [copy(d2_rows(xm(d)), d2_rows(xm(d)), SEM_AT["hand"] + i, core) for i, d in enumerate(X_PEERS)]
    swaps[3].wait_recv()
    start(t_z)
    swaps[1].wait_recv()
    start(r1_x)
    start(blocks)
    zr1[0, 0] = rt[1]

    def d_block(level, index):
        return dm[:, pl.ds(at(D_AT[level] + index * UNIT), UNIT)]

    def e_block(level, index):
        return em[:, pl.ds(at(E_AT[level] + index * UNIT), UNIT)]

    def pair_index(px, d):
        return lax.rem(xp if px else x, 2) * NZ + zm(d)

    loads[0].wait()
    swaps[4].wait_recv()

    def solve0(ch):
        total = nt(rt[0, cols(ch), :], d_block(0, z))
        for i, d in enumerate(Z_PEERS):
            gather_r0(ch)[i].wait_recv()
            total += nt(a0r[ch, i], d_block(0, zm(d)))
        s0b[ch] = total.astype(BF16)
        start(gather_z("a1", s0b, a1r, ch))

    chains(solve0)

    received(t_z)
    start(t_x)
    received(r1_x)
    start(r1_z)

    loads[1].wait()
    swaps[5].wait_recv()

    def update0(ch):
        total = nt(s0b[ch], e_block(0, z))
        copies = gather_z("a1", s0b, a1r, ch)
        for i, d in enumerate(Z_PEERS):
            copies[i].wait_recv()
            total += nt(a1r[ch, i], e_block(0, zm(d)))
        u0b[ch] = total.astype(BF16)
        start(gather_pair("u0", u0b, u0r, ch))

    chains(update0)

    def fill_select(target, base, count):
        for k in range(count):
            rows = lax.broadcasted_iota(jnp.int32, (UNIT, UNIT), 0) + (base + k * UNIT)
            select[k * UNIT : (k + 1) * UNIT, :] = jnp.where(rows == target, 1.0, 0.0).astype(BF16)

    loads[2].wait()
    swaps[6].wait_recv()
    received(t_x)

    def select1(j, carry):
        px, d = j // NZ, lax.rem(j, NZ)
        dx = px * (3 - 2 * xpar)
        source = lax.rem(x + px, 2) * NZ + zm(d)
        target = tg[dx, d, 0:1, :]
        total = jnp.zeros((UNIT, UNIT), F32)
        for part in range(2):
            fill_select(target, part * LEAF, 4)
            total += nn(dm[:, D_AT[1] + part * LEAF : D_AT[1] + (part + 1) * LEAF], select[...])
        m1[:, pl.ds(at(source * UNIT), UNIT)] = total.astype(BF16)
        return carry

    lax.fori_loop(0, 2 * NZ, select1, 0)
    received(r1_z)

    def rhs1(ch):
        total = jnp.zeros((WIDTH, UNIT), F32)
        for px in range(2):
            for d in range(NZ):
                total += nt(zr1[px, d, cols(ch), :], d_block(1, pair_index(px, d)))
        y1[ch] = total

    chains(rhs1)

    def solve1(ch):
        total = nt(u0b[ch], m1[:, pl.ds(at((xpar * NZ + z) * UNIT), UNIT)])
        copies = gather_pair("u0", u0b, u0r, ch)
        for i, (px, d) in reversed(list(enumerate(PAIR_PEERS))):
            copies[i].wait_recv()
            total += nt(u0r[ch, i], m1[:, pl.ds(at(pair_index(px, d) * UNIT), UNIT)])
        s1b[ch] = (y1[ch] - total).astype(BF16)
        start(gather_pair("s1", s1b, s1r, ch))

    chains(solve1)

    swaps[2].wait_recv()
    start(r2_z)
    for i in range(3):
        blocks[i].wait_recv()
        hands[i].start()
    loads[4].wait()
    swaps[8].wait_recv()
    received(hands)

    def select2(j, carry):
        side, zz = j // NZ, lax.rem(j, NZ)
        dx = lax.rem(x // 2 + side, 2) * 2
        target = tg[dx, lax.rem(z + NZ - zz, NZ), 1:2, :]
        fill_select(target, x * LEAF, 4)
        for k in range(NX):
            chosen = nn(d2[k * UNIT : (k + 1) * UNIT, :], select[...])
            m2[k * UNIT : (k + 1) * UNIT, pl.ds(at(j * UNIT), UNIT)] = chosen.astype(BF16)
        return carry

    lax.fori_loop(0, 4, select2, 0)

    loads[3].wait()
    swaps[7].wait_recv()

    def update1(ch):
        total = nt(s1b[ch], e_block(1, xpar * NZ + z))
        copies = gather_pair("s1", s1b, s1r, ch)
        for i, (px, d) in reversed(list(enumerate(PAIR_PEERS))):
            copies[i].wait_recv()
            total += nt(s1r[ch, i], e_block(1, pair_index(px, d)))
        u1b[ch] = total.astype(BF16)
        start(gather_skip("u1", u1b, u1r, ch))

    chains(update1)

    lax.fori_loop(4, 8, select2, 0)
    received(r2_z)

    def rhs2(ch):
        total = nt(rt[2, cols(ch), :], d2[:, pl.ds(at(z * UNIT), UNIT)])
        for d in range(1, NZ):
            total += nt(zr2[d, cols(ch), :], d2[:, pl.ds(at(zm(d) * UNIT), UNIT)])
        y2[ch] = total

    chains(rhs2)

    def spread(matrix, base, vector, dst, ch, leaves):
        for k in range(leaves):
            part = nn(vector, matrix[:, base + k * LEAF : base + (k + 1) * LEAF]).astype(BF16)
            for i in range(NZ):
                if leaves == 1:
                    dst[ch, i] = part[:, i * UNIT : (i + 1) * UNIT]
                else:
                    dst[ch, k, i] = part[:, i * UNIT : (i + 1) * UNIT]

    def skip_columns(px, d):
        return m2[:, pl.ds(at(((xo if px else x) // 2 * NZ + zm(d)) * UNIT), UNIT)]

    def solve2(ch):
        total = y2[ch] - nt(u1b[ch], skip_columns(0, 0))
        copies = gather_skip("u1", u1b, u1r, ch)
        for i, (px, d) in reversed(list(enumerate(PAIR_PEERS))):
            copies[i].wait_recv()
            total -= nt(u1r[ch, i], skip_columns(px, d))
        part = total.astype(BF16)
        for k in range(NX):
            s2rs[ch, k] = part[:, k * UNIT : (k + 1) * UNIT]
        start(reduce_x("s2r", s2rs, s2rr, ch))

    chains(solve2)

    def summed(copies, own, dst, ch):
        total = own.astype(F32)
        for i in reversed(range(len(copies))):
            copies[i].wait_recv()
            total += dst[ch, i].astype(F32)
        return total

    def share2(ch):
        s2b[ch] = summed(reduce_x("s2r", s2rs, s2rr, ch), s2rs[ch, x], s2rr, ch).astype(BF16)
        start(gather_x("s2a", s2b, s2ar, ch))

    chains(share2)

    def row_block(matrix, index, first, count):
        return matrix[pl.ds(at(index * UNIT), UNIT), first : first + count]

    def fetch2(ch):
        copies = gather_x("s2a", s2b, s2ar, ch)
        received(copies)
        for side in range(2):
            total = nn(s2b[ch], row_block(m2, x, side * LEAF, LEAF))
            for i, d in enumerate(X_PEERS):
                total += nn(s2ar[ch, i], row_block(m2, xm(d), side * LEAF, LEAF))
            part = total.astype(BF16)
            for i in range(NZ):
                f1s[ch, side, i] = part[:, i * UNIT : (i + 1) * UNIT]
        start(reduce_skip("f1", f1s, f1r, ch))

    chains(fetch2)

    def back2(ch):
        total = nn(s2b[ch], row_block(d2, x, 0, LEAF))
        for i, d in enumerate(X_PEERS):
            total += nn(s2ar[ch, i], row_block(d2, xm(d), 0, LEAF))
        part = total.astype(BF16)
        for i in range(NZ):
            d2zs[ch, i] = part[:, i * UNIT : (i + 1) * UNIT]
        start(reduce_z("d2z", d2zs, d2zr, ch))

    chains(back2)

    def out_copies(level):
        keep = pltpu.make_async_copy(stage_own.at[level], out_hbm.at[level, :, mine], lsem.at[6 + level])
        hand = copy(stage_other.at[level], out_hbm.at[level, :, mine], SEM_AT["out"] + level, core)
        return keep, hand

    def finish(level, name, src, dst):
        def one(ch):
            sol[level, cols(ch), :] = summed(reduce_z(name, src, dst, ch), src[ch, z], dst, ch)

        chains(one)
        stage_other[level] = sol[level, :, theirs].T
        keep, hand = out_copies(level)
        hand.start()
        stage_own[level] = sol[level, :, mine].T
        keep.start()

    def fetch1(ch):
        fetched = summed(reduce_skip("f1", f1s, f1r, ch), f1s[ch, x // 2, z], f1r, ch).astype(BF16)
        spread(em, E_AT[1], fetched, e1s, ch, 2)
        start(reduce_pair("e1", e1s, e1r, ch))

    chains(fetch1)

    def weigh1(ch):
        carried = summed(reduce_pair("e1", e1s, e1r, ch), e1s[ch, xpar, z], e1r, ch)
        weights = (s1b[ch].astype(F32) - carried).astype(BF16)
        w1b[ch] = weights
        spread(m1, 0, weights, f0s, ch, 2)
        start(reduce_pair("f0", f0s, f0r, ch))

    chains(weigh1)

    def back1(ch):
        spread(dm, D_AT[1], w1b[ch], d1xs, ch, 2)
        start(x_pair("d1x", d1xs, d1xr, ch))

    chains(back1)
    finish(2, "d2z", d2zs, d2zr)

    def fetch0(ch):
        fetched = summed(reduce_pair("f0", f0s, f0r, ch), f0s[ch, xpar, z], f0r, ch).astype(BF16)
        spread(em, E_AT[0], fetched, w0s, ch, 1)
        start(reduce_z("w0", w0s, w0r, ch))

    chains(fetch0)

    def back1z(ch):
        received(x_pair("d1x", d1xs, d1xr, ch))
        for k in range(NZ):
            d1zs[ch, k] = (d1xs[ch, xpar, k].astype(F32) + d1xr[ch, 0, k].astype(F32)).astype(BF16)
        start(reduce_z("d1z", d1zs, d1zr, ch))

    chains(back1z)

    def weigh0(ch):
        carried = summed(reduce_z("w0", w0s, w0r, ch), w0s[ch, z], w0r, ch)
        weights = (s0b[ch].astype(F32) - carried).astype(BF16)
        spread(dm, D_AT[0], weights, l0s, ch, 1)
        start(reduce_z("l0", l0s, l0r, ch))

    chains(weigh0)
    finish(1, "d1z", d1zs, d1zr)

    sent(swaps + blocks + hands + t_z + t_x + r1_x + r1_z + r2_z)

    def all_sent(ch):
        sent(gather_r0(ch))
        sent(gather_z("a1", s0b, a1r, ch))
        sent(gather_pair("u0", u0b, u0r, ch))
        sent(gather_pair("s1", s1b, s1r, ch))
        sent(gather_skip("u1", u1b, u1r, ch))
        sent(reduce_x("s2r", s2rs, s2rr, ch))
        sent(gather_x("s2a", s2b, s2ar, ch))
        sent(reduce_skip("f1", f1s, f1r, ch))
        sent(reduce_z("d2z", d2zs, d2zr, ch))
        sent(reduce_pair("e1", e1s, e1r, ch))
        sent(reduce_pair("f0", f0s, f0r, ch))
        sent(x_pair("d1x", d1xs, d1xr, ch))
        sent(reduce_z("d1z", d1zs, d1zr, ch))
        sent(reduce_z("w0", w0s, w0r, ch))

    chains(all_sent)

    finish(0, "l0", l0s, l0r)
    chains(lambda ch: sent(reduce_z("l0", l0s, l0r, ch)))
    for level in range(3):
        keep, hand = out_copies(level)
        keep.wait()
        hand.wait()


def shards(rhs, inverse_blocks, update_blocks, asm_owner, asm_row):
    k, w = CHAINS, WIDTH
    vmem = pl.BlockSpec(memory_space=pltpu.VMEM)
    hbm = pl.BlockSpec(memory_space=pl.ANY)
    block = lambda *lead: pltpu.VMEM((k, *lead, w, UNIT), BF16)
    return pl.pallas_call(
        kernel,
        out_shape=jax.ShapeDtypeStruct(rhs.shape, F32),
        in_specs=[vmem, vmem, hbm, hbm, hbm],
        out_specs=hbm,
        scratch_shapes=[
            pltpu.VMEM((3, ROW, 2 * HALF), BF16),
            pltpu.VMEM((UNIT, 3 * LEAF), BF16),
            pltpu.VMEM((LEAF, LEAF), BF16),
            pltpu.VMEM((UNIT, 3 * LEAF), BF16),
            pltpu.VMEM((UNIT, 2 * LEAF), BF16),
            pltpu.VMEM((LEAF, 2 * LEAF), BF16),
            pltpu.VMEM((3, HALF, ROW), BF16),
            pltpu.VMEM((3, HALF, UNIT), BF16),
            pltpu.VMEM((NX, NZ, 8, UNIT), jnp.int32),
            pltpu.VMEM((2, NZ, HALF, UNIT), BF16),
            pltpu.VMEM((NZ, HALF, UNIT), BF16),
            pltpu.VMEM((LEAF, UNIT), BF16),
            block(), block(), block(), block(), block(), block(),
            block(3), block(3), block(7), block(7), block(7),
            pltpu.VMEM((k, w, UNIT), F32),
            pltpu.VMEM((k, w, LEAF), F32),
            block(4), block(3), block(3),
            block(2, 4), block(7), block(2, 4), block(7), block(2, 4), block(7),
            block(4), block(3), block(4), block(3),
            block(4), block(3),
            block(2, 4), block(1, 4), block(4), block(3),
            pltpu.VMEM((3, HALF, UNIT), F32),
            pltpu.VMEM((3, ROW, HALF), F32),
            pltpu.VMEM((3, ROW, HALF), F32),
            pltpu.SemaphoreType.DMA((SEM_COUNT,)),
            pltpu.SemaphoreType.DMA((SEM_COUNT,)),
            pltpu.SemaphoreType.DMA((9,)),
        ],
        compiler_params=pltpu.CompilerParams(collective_id=0, has_side_effects=True, vmem_limit_bytes=56 * 2**20),
    )(asm_owner.reshape(asm_row.shape[0], 1, asm_row.shape[1]), asm_row, rhs, inverse_blocks, update_blocks)


def solution(mesh):
    placed = (
        P(None, ("leaf", "front"), None),
        P(("leaf", "front"), None),
        P(("leaf", "front"), None),
        P(None, ("leaf", "front"), None),
        P(None, ("leaf", "front")),
    )
    return jax.shard_map(
        shards, mesh=mesh, in_specs=placed, out_specs=P(None, ("leaf", "front"), None), check_vma=False
    )
```

```python
import functools

import jax
import jax.numpy as jnp
from jax import lax
from jax.experimental import pallas as pl
from jax.experimental.pallas import tpu as pltpu
from jax.sharding import PartitionSpec as P

MESH = pl.DeviceIdType.MESH
F32, BF16 = jnp.float32, jnp.bfloat16

CHAINS = 2
ROW = 128
UNIT = 256
HALF = 128
NX, NZ = 4, 4
LEAF = UNIT * NZ
WIDTH = HALF // CHAINS
D_AT = (0, LEAF)
E_AT = (0, LEAF)

Z_PEERS = (2, 1, 3)
PAIR_PEERS = ((1, 2), (1, 1), (1, 3), (0, 2), (1, 0), (0, 1), (0, 3))
X_PEERS = (2, 1, 3)
QUAD_PEERS = tuple((dx, dz) for dx in (2, 1, 3, 0) for dz in (2, 1, 3, 0) if dx or dz)

CHAINED = (
    ("a1", 3), ("u0", 7), ("s1", 7), ("u1", 7), ("s2r", 3), ("s2a", 3), ("f1", 7), ("e1", 7), ("f0", 7),
    ("w0", 3), ("l0", 3), ("d2z", 3), ("d1x", 1), ("d1z", 3),
)
SINGLE = (("a0", 3), ("a0x", 3), ("core", 9), ("block", 3), ("hand", 3), ("tz", 3), ("tx", 3), ("r1z", 3), ("r1x", 1), ("r2z", 3), ("out", 3))
SEM_AT, SEM_COUNT = {}, 0
for _name, _n in CHAINED:
    SEM_AT[_name] = SEM_COUNT
    SEM_COUNT += _n * CHAINS
for _name, _n in SINGLE:
    SEM_AT[_name] = SEM_COUNT
    SEM_COUNT += _n


def nt(left, right):
    return lax.dot_general(left, right, (((1,), (1,)), ((), ())), preferred_element_type=F32)


def nn(left, right):
    return lax.dot_general(left, right, (((1,), (0,)), ((), ())), preferred_element_type=F32)


def kernel(
    owner_hbm, row_hbm, rhs_hbm, d_hbm, e_hbm, out_hbm,
    owner_ref, row_ref, rhs_v, dm, d2, em, m1, m2, swap, rt, tg, zr1, zr2, select,
    s0b, u0b, s1b, u1b, s2b, w1b,
    a0, a1r, u0r, s1r, u1r, y1, y2, s2rs, s2rr, s2ar,
    f1s, f1r, e1s, e1r, f0s, f0r, w0s, w0r, l0s, l0r,
    d2zs, d2zr, d1xs, d1xr, d1zs, d1zr,
    sol, stage_own, stage_other,
    ssem, rsem, lsem,
):
    leaf, front = lax.axis_index("leaf"), lax.axis_index("front")
    x, y = lax.rem(leaf, NX), leaf // NX
    z, c = front // 2, lax.rem(front, 2)
    other = 1 - c
    xp = x + 1 - 2 * lax.rem(x, 2)
    xpar = lax.rem(x, 2)
    xo = lax.rem(x + 2, NX)

    def dev(xx, zz):
        return (y * NX + xx, zz * 2 + c)

    core = (leaf, z * 2 + other)

    def dev_other(zz):
        return (leaf, zz * 2 + other)

    def zp(d):
        return lax.rem(z + d, NZ)

    def zm(d):
        return lax.rem(z + NZ - d, NZ)

    def xq(d):
        return lax.rem(x + d, NX)

    def xm(d):
        return lax.rem(x + NX - d, NX)

    def at(value):
        return pl.multiple_of(value, UNIT)

    def copy(src, dst, sem, device):
        return pltpu.make_async_remote_copy(
            src_ref=src, dst_ref=dst, send_sem=ssem.at[sem], recv_sem=rsem.at[sem], device_id=device, device_id_type=MESH
        )

    def chains(body):
        def step(ch, carry):
            body(ch)
            return carry

        lax.fori_loop(0, CHAINS, step, 0)

    def cols(ch):
        return pl.ds(pl.multiple_of(ch * WIDTH, WIDTH), WIDTH)

    def gather_z(name, src, dst, ch):
        return [copy(src.at[ch], dst.at[ch, i], SEM_AT[name] + ch * 3 + i, dev(x, zp(d))) for i, d in enumerate(Z_PEERS)]

    def gather_pair(name, src, dst, ch):
        return [
            copy(src.at[ch], dst.at[ch, i], SEM_AT[name] + ch * 7 + i, dev(xp if px else x, zp(d)))
            for i, (px, d) in enumerate(PAIR_PEERS)
        ]

    def gather_skip(name, src, dst, ch):
        return [
            copy(src.at[ch], dst.at[ch, i], SEM_AT[name] + ch * 7 + i, dev(xo if px else x, zp(d)))
            for i, (px, d) in enumerate(PAIR_PEERS)
        ]

    def gather_x(name, src, dst, ch):
        return [copy(src.at[ch], dst.at[ch, i], SEM_AT[name] + ch * 3 + i, dev(xq(d), z)) for i, d in enumerate(X_PEERS)]

    def reduce_z(name, src, dst, ch):
        return [
            copy(src.at[ch, zp(d)], dst.at[ch, i], SEM_AT[name] + ch * 3 + i, dev(x, zp(d))) for i, d in enumerate(Z_PEERS)
        ]

    def reduce_pair(name, src, dst, ch):
        out = []
        for i, (px, d) in enumerate(PAIR_PEERS):
            xx = xp if px else x
            out.append(copy(src.at[ch, lax.rem(xx, 2), zp(d)], dst.at[ch, i], SEM_AT[name] + ch * 7 + i, dev(xx, zp(d))))
        return out

    def reduce_skip(name, src, dst, ch):
        out = []
        for i, (px, d) in enumerate(PAIR_PEERS):
            xx = xo if px else x
            out.append(copy(src.at[ch, xx // 2, zp(d)], dst.at[ch, i], SEM_AT[name] + ch * 7 + i, dev(xx, zp(d))))
        return out

    def reduce_x(name, src, dst, ch):
        return [copy(src.at[ch, xq(d)], dst.at[ch, i], SEM_AT[name] + ch * 3 + i, dev(xq(d), z)) for i, d in enumerate(X_PEERS)]

    def x_pair(name, src, dst, ch):
        return [copy(src.at[ch, 1 - xpar], dst.at[ch, 0], SEM_AT[name] + ch, dev(xp, z))]

    def start(copies):
        for one in copies:
            one.start()

    def received(copies):
        for one in copies:
            one.wait_recv()

    def sent(copies):
        for one in copies:
            one.wait_send()

    mine, theirs = pl.ds(pl.multiple_of(c * ROW, ROW), ROW), pl.ds(pl.multiple_of(other * ROW, ROW), ROW)
    spans = ((d_hbm, dm, 0, LEAF), (e_hbm, em, 0, LEAF), (d_hbm, dm, LEAF, 2 * LEAF), (e_hbm, em, LEAF, 2 * LEAF))

    def d2_columns(leaf_x):
        return d_hbm.at[:, pl.ds(pl.multiple_of((3 + leaf_x) * LEAF, LEAF), LEAF)]

    def d2_rows(leaf_x):
        return d2.at[pl.ds(pl.multiple_of(leaf_x * UNIT + c * ROW, ROW), ROW)]

    load_rhs = [pltpu.make_async_copy(rhs_hbm.at[level], rhs_v.at[level], lsem.at[9 + level]) for level in range(3)]
    load_lists = [
        pltpu.make_async_copy(owner_hbm, owner_ref, lsem.at[12]), pltpu.make_async_copy(row_hbm, row_ref, lsem.at[0])
    ]
    for one in load_rhs + load_lists:
        one.start()
    loads = [
        pltpu.make_async_copy(src.at[:, pl.ds(a, n)], dst.at[mine, pl.ds(a, n)], lsem.at[1 + i])
        for i, (src, dst, a, n) in enumerate(spans)
    ]
    loads.append(pltpu.make_async_copy(d2_columns(x), d2_rows(x), lsem.at[5]))
    for one in loads:
        one.start()
    barrier = pltpu.get_barrier_semaphore()
    pl.semaphore_signal(barrier, inc=1, device_id=core, device_id_type=MESH)
    for dx, d in QUAD_PEERS:
        pl.semaphore_signal(barrier, inc=1, device_id=dev(xq(dx), zp(d)), device_id_type=MESH)
    for d in Z_PEERS:
        pl.semaphore_signal(barrier, inc=1, device_id=dev_other(zp(d)), device_id_type=MESH)

    def turn(level, own):
        load_rhs[level].wait()
        swap[level] = rhs_v[level, :, theirs].astype(F32).T.astype(BF16)
        own[:, mine] = rhs_v[level, :, mine].astype(F32).T.astype(BF16)

    turn(0, a0.at[0])
    pl.semaphore_wait(barrier, 19)
    half = a0.at[0, :, mine]
    r0_same = [copy(half, a0.at[d, :, mine], SEM_AT["a0"] + i, dev(x, zp(d))) for i, d in enumerate(Z_PEERS)]
    r0_cross = [copy(swap.at[0], a0.at[d, :, mine], SEM_AT["a0x"] + i, dev_other(zp(d))) for i, d in enumerate(Z_PEERS)]
    for i in range(3):
        r0_same[i].start()
        r0_cross[i].start()
    swaps = [copy(swap.at[0], half, SEM_AT["core"], core)]
    swaps += [copy(swap.at[level], rt.at[level, :, mine], SEM_AT["core"] + level, core) for level in (1, 2)]
    swaps.append(copy(tg.at[0, 0, :, mine], tg.at[0, 0, :, mine], SEM_AT["core"] + 3, core))
    swaps += [
        copy(src.at[:, pl.ds(a, n)], dst.at[mine, pl.ds(a, n)], SEM_AT["core"] + 4 + i, core)
        for i, (src, dst, a, n) in enumerate(spans)
    ]
    swaps.append(copy(d2_columns(x), d2_rows(x), SEM_AT["core"] + 8, core))
    swaps[0].start()
    swaps[4].start()
    turn(1, rt.at[1])
    swaps[1].start()
    swaps[5].start()

    for one in load_lists:
        one.wait()
    for level in range(2):
        owner = owner_ref[level]
        row = row_ref[level : level + 1, :]
        if level == 0:
            target = owner * ROW + row
        else:
            target = xpar * LEAF + (owner // 8) * (2 * LEAF) + lax.rem(owner, 8) * ROW + row
        tg[0, 0, level : level + 1, mine] = target
    swaps[3].start()
    turn(2, rt.at[2])
    swaps[2].start()
    for i in (6, 7, 8):
        swaps[i].start()

    t_z = [copy(tg.at[0, 0], tg.at[0, d], SEM_AT["tz"] + i, dev(x, zp(d))) for i, d in enumerate(Z_PEERS)]
    t_x = [copy(tg.at[0], tg.at[d], SEM_AT["tx"] + i, dev(xq(d), z)) for i, d in enumerate(Z_PEERS)]
    r1_x = [copy(rt.at[1], zr1.at[1, 0], SEM_AT["r1x"], dev(xp, z))]
    r1_z = [copy(zr1.at[:, 0], zr1.at[:, d], SEM_AT["r1z"] + i, dev(x, zp(d))) for i, d in enumerate(Z_PEERS)]
    r2_z = [copy(rt.at[2], zr2.at[d], SEM_AT["r2z"] + i, dev(x, zp(d))) for i, d in enumerate(Z_PEERS)]
    blocks = [copy(d2_columns(xq(d)), d2_rows(x), SEM_AT["block"] + i, dev(xq(d), z)) for i, d in enumerate(X_PEERS)]
    hands = [copy(d2_rows(xm(d)), d2_rows(xm(d)), SEM_AT["hand"] + i, core) for i, d in enumerate(X_PEERS)]
    swaps[3].wait_recv()
    start(t_z)
    swaps[1].wait_recv()
    start(r1_x)
    start(blocks)
    zr1[0, 0] = rt[1]

    def d_block(level, index):
        return dm[:, pl.ds(at(D_AT[level] + index * UNIT), UNIT)]

    def e_block(level, index):
        return em[:, pl.ds(at(E_AT[level] + index * UNIT), UNIT)]

    def pair_index(px, d):
        return lax.rem(xp if px else x, 2) * NZ + zm(d)

    loads[0].wait()
    swaps[4].wait_recv()

    def solve0(ch):
        total = nt(a0[0, cols(ch), :], d_block(0, z))
        for d in range(1, NZ):
            total += nt(a0[d, cols(ch), :], d_block(0, zm(d)))
        s0b[ch] = total.astype(BF16)
        start(gather_z("a1", s0b, a1r, ch))

    swaps[0].wait_recv()
    received(r0_same + r0_cross)
    chains(solve0)

    received(t_z)
    start(t_x)
    received(r1_x)
    start(r1_z)

    def fill_select(target, base, count):
        for k in range(count):
            rows = lax.broadcasted_iota(jnp.int32, (UNIT, UNIT), 0) + (base + k * UNIT)
            select[k * UNIT : (k + 1) * UNIT, :] = jnp.where(rows == target, 1.0, 0.0).astype(BF16)

    def select1(j, carry):
        px, d = j // NZ, lax.rem(j, NZ)
        dx = px * (3 - 2 * xpar)
        source = lax.rem(x + px, 2) * NZ + zm(d)
        target = tg[dx, d, 0:1, :]
        total = jnp.zeros((UNIT, UNIT), F32)
        for part in range(2):
            fill_select(target, part * LEAF, 4)
            total += nn(dm[:, D_AT[1] + part * LEAF : D_AT[1] + (part + 1) * LEAF], select[...])
        m1[:, pl.ds(at(source * UNIT), UNIT)] = total.astype(BF16)
        return carry

    loads[2].wait()
    swaps[6].wait_recv()
    lax.fori_loop(0, 3, select1, 0)
    loads[1].wait()
    swaps[5].wait_recv()

    def update0(ch):
        total = nt(s0b[ch], e_block(0, z))
        copies = gather_z("a1", s0b, a1r, ch)
        for i, d in enumerate(Z_PEERS):
            copies[i].wait_recv()
            total += nt(a1r[ch, i], e_block(0, zm(d)))
        u0b[ch] = total.astype(BF16)
        start(gather_pair("u0", u0b, u0r, ch))

    chains(update0)

    received(t_x)

    lax.fori_loop(3, 2 * NZ, select1, 0)
    received(r1_z)

    def rhs1(ch):
        total = jnp.zeros((WIDTH, UNIT), F32)
        for px in range(2):
            for d in range(NZ):
                total += nt(zr1[px, d, cols(ch), :], d_block(1, pair_index(px, d)))
        y1[ch] = total

    chains(rhs1)

    def solve1(ch):
        total = nt(u0b[ch], m1[:, pl.ds(at((xpar * NZ + z) * UNIT), UNIT)])
        copies = gather_pair("u0", u0b, u0r, ch)
        for i, (px, d) in reversed(list(enumerate(PAIR_PEERS))):
            copies[i].wait_recv()
            total += nt(u0r[ch, i], m1[:, pl.ds(at(pair_index(px, d) * UNIT), UNIT)])
        s1b[ch] = (y1[ch] - total).astype(BF16)
        start(gather_pair("s1", s1b, s1r, ch))

    chains(solve1)

    swaps[2].wait_recv()
    start(r2_z)
    for i in range(3):
        blocks[i].wait_recv()
        hands[i].start()
    loads[4].wait()
    swaps[8].wait_recv()
    received(hands)

    def select2(j, carry):
        side, zz = j // NZ, lax.rem(j, NZ)
        dx = lax.rem(x // 2 + side, 2) * 2
        target = tg[dx, lax.rem(z + NZ - zz, NZ), 1:2, :]
        fill_select(target, x * LEAF, 4)
        m2[:, pl.ds(at(j * UNIT), UNIT)] = nn(d2[...], select[...]).astype(BF16)
        return carry

    lax.fori_loop(0, 4, select2, 0)

    loads[3].wait()
    swaps[7].wait_recv()

    def update1(ch):
        total = nt(s1b[ch], e_block(1, xpar * NZ + z))
        copies = gather_pair("s1", s1b, s1r, ch)
        for i, (px, d) in reversed(list(enumerate(PAIR_PEERS))):
            copies[i].wait_recv()
            total += nt(s1r[ch, i], e_block(1, pair_index(px, d)))
        u1b[ch] = total.astype(BF16)
        start(gather_skip("u1", u1b, u1r, ch))

    chains(update1)

    lax.fori_loop(4, 8, select2, 0)
    received(r2_z)

    def rhs2(ch):
        total = nt(rt[2, cols(ch), :], d2[:, pl.ds(at(z * UNIT), UNIT)])
        for d in range(1, NZ):
            total += nt(zr2[d, cols(ch), :], d2[:, pl.ds(at(zm(d) * UNIT), UNIT)])
        y2[ch] = total

    chains(rhs2)

    def spread(matrix, base, vector, dst, ch, leaves):
        for k in range(leaves):
            part = nn(vector, matrix[:, base + k * LEAF : base + (k + 1) * LEAF]).astype(BF16)
            for i in range(NZ):
                if leaves == 1:
                    dst[ch, i] = part[:, i * UNIT : (i + 1) * UNIT]
                else:
                    dst[ch, k, i] = part[:, i * UNIT : (i + 1) * UNIT]

    def skip_columns(px, d):
        return m2[:, pl.ds(at(((xo if px else x) // 2 * NZ + zm(d)) * UNIT), UNIT)]

    def solve2(ch):
        total = y2[ch] - nt(u1b[ch], skip_columns(0, 0))
        copies = gather_skip("u1", u1b, u1r, ch)
        for i, (px, d) in reversed(list(enumerate(PAIR_PEERS))):
            copies[i].wait_recv()
            total -= nt(u1r[ch, i], skip_columns(px, d))
        part = total.astype(BF16)
        for k in range(NX):
            s2rs[ch, k] = part[:, k * UNIT : (k + 1) * UNIT]
        start(reduce_x("s2r", s2rs, s2rr, ch))

    chains(solve2)

    def summed(copies, own, dst, ch):
        total = own.astype(F32)
        for i in reversed(range(len(copies))):
            copies[i].wait_recv()
            total += dst[ch, i].astype(F32)
        return total

    def share2(ch):
        s2b[ch] = summed(reduce_x("s2r", s2rs, s2rr, ch), s2rs[ch, x], s2rr, ch).astype(BF16)
        start(gather_x("s2a", s2b, s2ar, ch))

    chains(share2)
    sent(swaps + r0_same + r0_cross + blocks + hands + t_z + t_x + r1_x + r1_z + r2_z)

    def row_block(matrix, index, first, count):
        return matrix[pl.ds(at(index * UNIT), UNIT), first : first + count]

    def fetch2(ch):
        copies = gather_x("s2a", s2b, s2ar, ch)
        totals = [nn(s2b[ch], row_block(m2, x, side * LEAF, LEAF)) for side in range(2)]
        for i, d in reversed(list(enumerate(X_PEERS))):
            copies[i].wait_recv()
            for side in range(2):
                totals[side] += nn(s2ar[ch, i], row_block(m2, xm(d), side * LEAF, LEAF))
        for side in range(2):
            part = totals[side].astype(BF16)
            for i in range(NZ):
                f1s[ch, side, i] = part[:, i * UNIT : (i + 1) * UNIT]
        start(reduce_skip("f1", f1s, f1r, ch))

    chains(fetch2)

    def sent_forward(ch):
        sent(gather_z("a1", s0b, a1r, ch))
        sent(gather_pair("u0", u0b, u0r, ch))
        sent(gather_pair("s1", s1b, s1r, ch))
        sent(gather_skip("u1", u1b, u1r, ch))
        sent(reduce_x("s2r", s2rs, s2rr, ch))
        sent(gather_x("s2a", s2b, s2ar, ch))

    chains(sent_forward)

    def back2(ch):
        total = nn(s2b[ch], row_block(d2, x, 0, LEAF))
        for i, d in enumerate(X_PEERS):
            total += nn(s2ar[ch, i], row_block(d2, xm(d), 0, LEAF))
        part = total.astype(BF16)
        for i in range(NZ):
            d2zs[ch, i] = part[:, i * UNIT : (i + 1) * UNIT]
        start(reduce_z("d2z", d2zs, d2zr, ch))

    def out_copies(level):
        keep = pltpu.make_async_copy(stage_own.at[level], out_hbm.at[level, :, mine], lsem.at[6 + level])
        hand = copy(stage_other.at[level], out_hbm.at[level, :, mine], SEM_AT["out"] + level, core)
        return keep, hand

    def finish(level, name, src, dst):
        def one(ch):
            sol[level, cols(ch), :] = summed(reduce_z(name, src, dst, ch), src[ch, z], dst, ch)

        chains(one)
        stage_other[level] = sol[level, :, theirs].T
        keep, hand = out_copies(level)
        hand.start()
        stage_own[level] = sol[level, :, mine].T
        keep.start()

    def fetch1(ch):
        fetched = summed(reduce_skip("f1", f1s, f1r, ch), f1s[ch, x // 2, z], f1r, ch).astype(BF16)
        spread(em, E_AT[1], fetched, e1s, ch, 2)
        start(reduce_pair("e1", e1s, e1r, ch))

    chains(fetch1)
    chains(back2)

    def weigh1(ch):
        carried = summed(reduce_pair("e1", e1s, e1r, ch), e1s[ch, xpar, z], e1r, ch)
        weights = (s1b[ch].astype(F32) - carried).astype(BF16)
        w1b[ch] = weights
        spread(m1, 0, weights, f0s, ch, 2)
        start(reduce_pair("f0", f0s, f0r, ch))

    chains(weigh1)

    def back1(ch):
        spread(dm, D_AT[1], w1b[ch], d1xs, ch, 2)
        start(x_pair("d1x", d1xs, d1xr, ch))

    chains(back1)
    finish(2, "d2z", d2zs, d2zr)

    def fetch0(ch):
        fetched = summed(reduce_pair("f0", f0s, f0r, ch), f0s[ch, xpar, z], f0r, ch).astype(BF16)
        spread(em, E_AT[0], fetched, w0s, ch, 1)
        start(reduce_z("w0", w0s, w0r, ch))

    chains(fetch0)

    def back1z(ch):
        received(x_pair("d1x", d1xs, d1xr, ch))
        for k in range(NZ):
            d1zs[ch, k] = (d1xs[ch, xpar, k].astype(F32) + d1xr[ch, 0, k].astype(F32)).astype(BF16)
        start(reduce_z("d1z", d1zs, d1zr, ch))

    chains(back1z)

    def weigh0(ch):
        carried = summed(reduce_z("w0", w0s, w0r, ch), w0s[ch, z], w0r, ch)
        weights = (s0b[ch].astype(F32) - carried).astype(BF16)
        spread(dm, D_AT[0], weights, l0s, ch, 1)
        start(reduce_z("l0", l0s, l0r, ch))

    chains(weigh0)

    def sent_adjoint(ch):
        sent(reduce_skip("f1", f1s, f1r, ch))
        sent(reduce_z("d2z", d2zs, d2zr, ch))
        sent(reduce_pair("e1", e1s, e1r, ch))
        sent(reduce_pair("f0", f0s, f0r, ch))
        sent(x_pair("d1x", d1xs, d1xr, ch))
        sent(reduce_z("w0", w0s, w0r, ch))

    chains(sent_adjoint)
    finish(1, "d1z", d1zs, d1zr)

    finish(0, "l0", l0s, l0r)

    def sent_last(ch):
        sent(reduce_z("d1z", d1zs, d1zr, ch))
        sent(reduce_z("l0", l0s, l0r, ch))

    chains(sent_last)
    for level in range(3):
        keep, hand = out_copies(level)
        keep.wait()
        hand.wait()


def shards(rhs, inverse_blocks, update_blocks, asm_owner, asm_row):
    k, w = CHAINS, WIDTH
    hbm = pl.BlockSpec(memory_space=pl.ANY)
    block = lambda *lead: pltpu.VMEM((k, *lead, w, UNIT), BF16)
    return pl.pallas_call(
        kernel,
        out_shape=jax.ShapeDtypeStruct(rhs.shape, F32),
        in_specs=[hbm] * 5,
        out_specs=hbm,
        scratch_shapes=[
            pltpu.VMEM((2, 1, ROW), jnp.int32),
            pltpu.VMEM((2, ROW), jnp.int32),
            pltpu.VMEM((3, ROW, 2 * HALF), BF16),
            pltpu.VMEM((UNIT, 3 * LEAF), BF16),
            pltpu.VMEM((LEAF, LEAF), BF16),
            pltpu.VMEM((UNIT, 3 * LEAF), BF16),
            pltpu.VMEM((UNIT, 2 * LEAF), BF16),
            pltpu.VMEM((LEAF, 2 * LEAF), BF16),
            pltpu.VMEM((3, HALF, ROW), BF16),
            pltpu.VMEM((3, HALF, UNIT), BF16),
            pltpu.VMEM((NX, NZ, 8, UNIT), jnp.int32),
            pltpu.VMEM((2, NZ, HALF, UNIT), BF16),
            pltpu.VMEM((NZ, HALF, UNIT), BF16),
            pltpu.VMEM((LEAF, UNIT), BF16),
            block(), block(), block(), block(), block(), block(),
            pltpu.VMEM((NZ, HALF, UNIT), BF16),
            block(3), block(7), block(7), block(7),
            pltpu.VMEM((k, w, UNIT), F32),
            pltpu.VMEM((k, w, LEAF), F32),
            block(4), block(3), block(3),
            block(2, 4), block(7), block(2, 4), block(7), block(2, 4), block(7),
            block(4), block(3), block(4), block(3),
            block(4), block(3),
            block(2, 4), block(1, 4), block(4), block(3),
            pltpu.VMEM((3, HALF, UNIT), F32),
            pltpu.VMEM((3, ROW, HALF), F32),
            pltpu.VMEM((3, ROW, HALF), F32),
            pltpu.SemaphoreType.DMA((SEM_COUNT,)),
            pltpu.SemaphoreType.DMA((SEM_COUNT,)),
            pltpu.SemaphoreType.DMA((13,)),
        ],
        compiler_params=pltpu.CompilerParams(collective_id=0, has_side_effects=True, vmem_limit_bytes=32 * 2**20),
    )(*[pltpu.with_memory_space_constraint(one, pltpu.HBM) for one in (asm_owner.reshape(asm_row.shape[0], 1, asm_row.shape[1]), asm_row, rhs, inverse_blocks, update_blocks)])


def solution(mesh):
    placed = (
        P(None, ("leaf", "front"), None),
        P(("leaf", "front"), None),
        P(("leaf", "front"), None),
        P(None, ("leaf", "front"), None),
        P(None, ("leaf", "front")),
    )
    return jax.shard_map(
        shards, mesh=mesh, in_specs=placed, out_specs=P(None, ("leaf", "front"), None), check_vma=False
    )
```

```python
import functools

import jax
import jax.numpy as jnp
from jax import lax
from jax.experimental import pallas as pl
from jax.experimental.pallas import tpu as pltpu
from jax.sharding import PartitionSpec as P

MESH = pl.DeviceIdType.MESH
F32, BF16 = jnp.float32, jnp.bfloat16

CHAINS = 2
ROW = 128
UNIT = 256
HALF = 128
NX, NZ = 4, 4
LEAF = UNIT * NZ
WIDTH = HALF // CHAINS
D_AT = (0, LEAF)
E_AT = (0, LEAF)

Z_PEERS = (2, 1, 3)
PAIR_PEERS = ((1, 2), (1, 1), (1, 3), (0, 2), (1, 0), (0, 1), (0, 3))
X_PEERS = (2, 1, 3)
QUAD_PEERS = tuple((dx, dz) for dx in (2, 1, 3, 0) for dz in (2, 1, 3, 0) if dx or dz)

CHAINED = (
    ("a1", 3), ("u0", 7), ("s1", 7), ("u1", 7), ("s2r", 3), ("s2a", 3), ("f1", 7), ("e1", 7), ("f0", 7),
    ("w0", 3), ("l0", 3), ("d2z", 3), ("d1x", 1), ("d1z", 3),
)
SINGLE = (("a0", 3), ("a0x", 3), ("core", 9), ("block", 3), ("hand", 3), ("tz", 3), ("tx", 3), ("r1z", 3), ("r1x", 1), ("r2z", 3), ("out", 3))
SEM_AT, SEM_COUNT = {}, 0
for _name, _n in CHAINED:
    SEM_AT[_name] = SEM_COUNT
    SEM_COUNT += _n * CHAINS
for _name, _n in SINGLE:
    SEM_AT[_name] = SEM_COUNT
    SEM_COUNT += _n


def nt(left, right):
    return lax.dot_general(left, right, (((1,), (1,)), ((), ())), preferred_element_type=F32)


def nn(left, right):
    return lax.dot_general(left, right, (((1,), (0,)), ((), ())), preferred_element_type=F32)


def kernel(
    owner_hbm, row_hbm, rhs_hbm, d_hbm, e_hbm, out_hbm,
    owner_ref, row_ref, rhs_v, dm, d2, em, m1, m2, swap, rt, tg, zr1, zr2, select,
    s0b, u0b, s1b, u1b, s2b, w1b,
    a0, a1r, u0r, s1r, u1r, y1, y2, s2rs, s2rr, s2ar,
    f1s, f1r, e1s, e1r, f0s, f0r, w0s, w0r, l0s, l0r,
    d2zs, d2zr, d1xs, d1xr, d1zs, d1zr,
    sol, stage_own, stage_other,
    ssem, rsem, lsem,
):
    leaf, front = lax.axis_index("leaf"), lax.axis_index("front")
    x, y = lax.rem(leaf, NX), leaf // NX
    z, c = front // 2, lax.rem(front, 2)
    other = 1 - c
    xp = x + 1 - 2 * lax.rem(x, 2)
    xpar = lax.rem(x, 2)
    xo = lax.rem(x + 2, NX)

    def dev(xx, zz):
        return (y * NX + xx, zz * 2 + c)

    core = (leaf, z * 2 + other)

    def dev_other(zz):
        return (leaf, zz * 2 + other)

    def zp(d):
        return lax.rem(z + d, NZ)

    def zm(d):
        return lax.rem(z + NZ - d, NZ)

    def xq(d):
        return lax.rem(x + d, NX)

    def xm(d):
        return lax.rem(x + NX - d, NX)

    def at(value):
        return pl.multiple_of(value, UNIT)

    def copy(src, dst, sem, device):
        return pltpu.make_async_remote_copy(
            src_ref=src, dst_ref=dst, send_sem=ssem.at[sem], recv_sem=rsem.at[sem], device_id=device, device_id_type=MESH
        )

    def chains(body):
        def step(ch, carry):
            body(ch)
            return carry

        lax.fori_loop(0, CHAINS, step, 0)

    def cols(ch):
        return pl.ds(pl.multiple_of(ch * WIDTH, WIDTH), WIDTH)

    def gather_z(name, src, dst, ch):
        return [copy(src.at[ch], dst.at[ch, i], SEM_AT[name] + ch * 3 + i, dev(x, zp(d))) for i, d in enumerate(Z_PEERS)]

    def gather_pair(name, src, dst, ch):
        return [
            copy(src.at[ch], dst.at[ch, i], SEM_AT[name] + ch * 7 + i, dev(xp if px else x, zp(d)))
            for i, (px, d) in enumerate(PAIR_PEERS)
        ]

    def gather_skip(name, src, dst, ch):
        return [
            copy(src.at[ch], dst.at[ch, i], SEM_AT[name] + ch * 7 + i, dev(xo if px else x, zp(d)))
            for i, (px, d) in enumerate(PAIR_PEERS)
        ]

    def gather_x(name, src, dst, ch):
        return [copy(src.at[ch], dst.at[ch, i], SEM_AT[name] + ch * 3 + i, dev(xq(d), z)) for i, d in enumerate(X_PEERS)]

    def reduce_z(name, src, dst, ch):
        return [
            copy(src.at[ch, zp(d)], dst.at[ch, i], SEM_AT[name] + ch * 3 + i, dev(x, zp(d))) for i, d in enumerate(Z_PEERS)
        ]

    def reduce_pair(name, src, dst, ch):
        out = []
        for i, (px, d) in enumerate(PAIR_PEERS):
            xx = xp if px else x
            out.append(copy(src.at[ch, lax.rem(xx, 2), zp(d)], dst.at[ch, i], SEM_AT[name] + ch * 7 + i, dev(xx, zp(d))))
        return out

    def reduce_skip(name, src, dst, ch):
        out = []
        for i, (px, d) in enumerate(PAIR_PEERS):
            xx = xo if px else x
            out.append(copy(src.at[ch, xx // 2, zp(d)], dst.at[ch, i], SEM_AT[name] + ch * 7 + i, dev(xx, zp(d))))
        return out

    def reduce_x(name, src, dst, ch):
        return [copy(src.at[ch, xq(d)], dst.at[ch, i], SEM_AT[name] + ch * 3 + i, dev(xq(d), z)) for i, d in enumerate(X_PEERS)]

    def x_pair(name, src, dst, ch):
        return [copy(src.at[ch, 1 - xpar], dst.at[ch, 0], SEM_AT[name] + ch, dev(xp, z))]

    def start(copies):
        for one in copies:
            one.start()

    def received(copies):
        for one in copies:
            one.wait_recv()

    def sent(copies):
        for one in copies:
            one.wait_send()

    mine, theirs = pl.ds(pl.multiple_of(c * ROW, ROW), ROW), pl.ds(pl.multiple_of(other * ROW, ROW), ROW)
    spans = ((d_hbm, dm, 0, LEAF), (e_hbm, em, 0, LEAF), (d_hbm, dm, LEAF, 2 * LEAF), (e_hbm, em, LEAF, 2 * LEAF))

    def d2_columns(leaf_x):
        return d_hbm.at[:, pl.ds(pl.multiple_of((3 + leaf_x) * LEAF, LEAF), LEAF)]

    def d2_rows(leaf_x):
        return d2.at[pl.ds(pl.multiple_of(leaf_x * UNIT + c * ROW, ROW), ROW)]

    load_rhs = [pltpu.make_async_copy(rhs_hbm.at[level], rhs_v.at[level], lsem.at[9 + level]) for level in range(3)]
    load_lists = [
        pltpu.make_async_copy(owner_hbm, owner_ref, lsem.at[12]), pltpu.make_async_copy(row_hbm, row_ref, lsem.at[0])
    ]
    for one in load_rhs + load_lists:
        one.start()
    loads = [
        pltpu.make_async_copy(src.at[:, pl.ds(a, n)], dst.at[mine, pl.ds(a, n)], lsem.at[1 + i])
        for i, (src, dst, a, n) in enumerate(spans)
    ]
    loads.append(pltpu.make_async_copy(d2_columns(x), d2_rows(x), lsem.at[5]))
    for one in loads:
        one.start()
    barrier = pltpu.get_barrier_semaphore()
    pl.semaphore_signal(barrier, inc=1, device_id=core, device_id_type=MESH)
    for dx, d in QUAD_PEERS:
        pl.semaphore_signal(barrier, inc=1, device_id=dev(xq(dx), zp(d)), device_id_type=MESH)
    for d in Z_PEERS:
        pl.semaphore_signal(barrier, inc=1, device_id=dev_other(zp(d)), device_id_type=MESH)

    def turn(level, own):
        load_rhs[level].wait()
        swap[level] = rhs_v[level, :, theirs].astype(F32).T.astype(BF16)
        own[:, mine] = rhs_v[level, :, mine].astype(F32).T.astype(BF16)

    turn(0, a0.at[0])
    pl.semaphore_wait(barrier, 19)
    half = a0.at[0, :, mine]
    r0_same = [copy(half, a0.at[d, :, mine], SEM_AT["a0"] + i, dev(x, zp(d))) for i, d in enumerate(Z_PEERS)]
    r0_cross = [copy(swap.at[0], a0.at[d, :, mine], SEM_AT["a0x"] + i, dev_other(zp(d))) for i, d in enumerate(Z_PEERS)]
    for i in range(3):
        r0_same[i].start()
        r0_cross[i].start()
    swaps = [copy(swap.at[0], half, SEM_AT["core"], core)]
    swaps += [copy(swap.at[level], rt.at[level, :, mine], SEM_AT["core"] + level, core) for level in (1, 2)]
    swaps.append(copy(tg.at[0, 0, :, mine], tg.at[0, 0, :, mine], SEM_AT["core"] + 3, core))
    swaps += [
        copy(src.at[:, pl.ds(a, n)], dst.at[mine, pl.ds(a, n)], SEM_AT["core"] + 4 + i, core)
        for i, (src, dst, a, n) in enumerate(spans)
    ]
    swaps.append(copy(d2_columns(x), d2_rows(x), SEM_AT["core"] + 8, core))
    swaps[0].start()
    swaps[4].start()
    turn(1, rt.at[1])
    swaps[1].start()
    swaps[5].start()

    for one in load_lists:
        one.wait()
    for level in range(2):
        owner = owner_ref[level]
        row = row_ref[level : level + 1, :]
        if level == 0:
            target = owner * ROW + row
        else:
            target = xpar * LEAF + (owner // 8) * (2 * LEAF) + lax.rem(owner, 8) * ROW + row
        tg[0, 0, level : level + 1, mine] = target
    swaps[3].start()
    turn(2, rt.at[2])
    swaps[2].start()
    for i in (6, 7, 8):
        swaps[i].start()

    t_z = [copy(tg.at[0, 0], tg.at[0, d], SEM_AT["tz"] + i, dev(x, zp(d))) for i, d in enumerate(Z_PEERS)]
    t_x = [copy(tg.at[0], tg.at[d], SEM_AT["tx"] + i, dev(xq(d), z)) for i, d in enumerate(Z_PEERS)]
    r1_x = [copy(rt.at[1], zr1.at[1, 0], SEM_AT["r1x"], dev(xp, z))]
    r1_z = [copy(zr1.at[:, 0], zr1.at[:, d], SEM_AT["r1z"] + i, dev(x, zp(d))) for i, d in enumerate(Z_PEERS)]
    r2_z = [copy(rt.at[2], zr2.at[d], SEM_AT["r2z"] + i, dev(x, zp(d))) for i, d in enumerate(Z_PEERS)]
    blocks = [copy(d2_columns(xq(d)), d2_rows(x), SEM_AT["block"] + i, dev(xq(d), z)) for i, d in enumerate(X_PEERS)]
    hands = [copy(d2_rows(xm(d)), d2_rows(xm(d)), SEM_AT["hand"] + i, core) for i, d in enumerate(X_PEERS)]
    swaps[3].wait_recv()
    start(t_z)
    swaps[1].wait_recv()
    start(r1_x)
    start(blocks[1:])
    zr1[0, 0] = rt[1]

    def d_block(level, index):
        return dm[:, pl.ds(at(D_AT[level] + index * UNIT), UNIT)]

    def e_block(level, index):
        return em[:, pl.ds(at(E_AT[level] + index * UNIT), UNIT)]

    def pair_index(px, d):
        return lax.rem(xp if px else x, 2) * NZ + zm(d)

    loads[0].wait()
    swaps[4].wait_recv()

    def solve0(ch):
        total = nt(a0[0, cols(ch), :], d_block(0, z))
        for d in range(1, NZ):
            total += nt(a0[d, cols(ch), :], d_block(0, zm(d)))
        s0b[ch] = total.astype(BF16)
        start(gather_z("a1", s0b, a1r, ch))

    swaps[0].wait_recv()
    received(r0_same + r0_cross)
    chains(solve0)
    start(blocks[:1])

    received(t_z)
    start(t_x)
    received(r1_x)
    start(r1_z)

    def fill_select(target, base, count):
        for k in range(count):
            rows = lax.broadcasted_iota(jnp.int32, (UNIT, UNIT), 0) + (base + k * UNIT)
            select[k * UNIT : (k + 1) * UNIT, :] = jnp.where(rows == target, 1.0, 0.0).astype(BF16)

    def select1(j, carry):
        px, d = j // NZ, lax.rem(j, NZ)
        dx = px * (3 - 2 * xpar)
        source = lax.rem(x + px, 2) * NZ + zm(d)
        target = tg[dx, d, 0:1, :]
        total = jnp.zeros((UNIT, UNIT), F32)
        for part in range(2):
            fill_select(target, part * LEAF, 4)
            total += nn(dm[:, D_AT[1] + part * LEAF : D_AT[1] + (part + 1) * LEAF], select[...])
        m1[:, pl.ds(at(source * UNIT), UNIT)] = total.astype(BF16)
        return carry

    loads[2].wait()
    swaps[6].wait_recv()
    lax.fori_loop(0, 3, select1, 0)
    loads[1].wait()
    swaps[5].wait_recv()

    def update0(ch):
        total = nt(s0b[ch], e_block(0, z))
        copies = gather_z("a1", s0b, a1r, ch)
        for i, d in enumerate(Z_PEERS):
            copies[i].wait_recv()
            total += nt(a1r[ch, i], e_block(0, zm(d)))
        u0b[ch] = total.astype(BF16)
        start(gather_pair("u0", u0b, u0r, ch))

    chains(update0)

    received(t_x)

    lax.fori_loop(3, 2 * NZ, select1, 0)
    received(r1_z)

    def rhs1(ch):
        total = jnp.zeros((WIDTH, UNIT), F32)
        for px in range(2):
            for d in range(NZ):
                total += nt(zr1[px, d, cols(ch), :], d_block(1, pair_index(px, d)))
        y1[ch] = total

    chains(rhs1)

    def solve1(ch):
        total = nt(u0b[ch], m1[:, pl.ds(at((xpar * NZ + z) * UNIT), UNIT)])
        copies = gather_pair("u0", u0b, u0r, ch)
        for i, (px, d) in reversed(list(enumerate(PAIR_PEERS))):
            copies[i].wait_recv()
            total += nt(u0r[ch, i], m1[:, pl.ds(at(pair_index(px, d) * UNIT), UNIT)])
        s1b[ch] = (y1[ch] - total).astype(BF16)
        start(gather_pair("s1", s1b, s1r, ch))

    chains(solve1)

    swaps[2].wait_recv()
    start(r2_z)
    for i in range(3):
        blocks[i].wait_recv()
        hands[i].start()
    loads[4].wait()
    swaps[8].wait_recv()
    received(hands)

    def select2(j, carry):
        side, zz = j // NZ, lax.rem(j, NZ)
        dx = lax.rem(x // 2 + side, 2) * 2
        target = tg[dx, lax.rem(z + NZ - zz, NZ), 1:2, :]
        fill_select(target, x * LEAF, 4)
        m2[:, pl.ds(at(j * UNIT), UNIT)] = nn(d2[...], select[...]).astype(BF16)
        return carry

    lax.fori_loop(0, 4, select2, 0)

    loads[3].wait()
    swaps[7].wait_recv()

    def update1(ch):
        total = nt(s1b[ch], e_block(1, xpar * NZ + z))
        copies = gather_pair("s1", s1b, s1r, ch)
        for i, (px, d) in reversed(list(enumerate(PAIR_PEERS))):
            copies[i].wait_recv()
            total += nt(s1r[ch, i], e_block(1, pair_index(px, d)))
        u1b[ch] = total.astype(BF16)
        start(gather_skip("u1", u1b, u1r, ch))

    chains(update1)

    lax.fori_loop(4, 8, select2, 0)
    received(r2_z)

    def rhs2(ch):
        total = nt(rt[2, cols(ch), :], d2[:, pl.ds(at(z * UNIT), UNIT)])
        for d in range(1, NZ):
            total += nt(zr2[d, cols(ch), :], d2[:, pl.ds(at(zm(d) * UNIT), UNIT)])
        y2[ch] = total

    chains(rhs2)

    def spread(matrix, base, vector, dst, ch, leaves):
        for k in range(leaves):
            part = nn(vector, matrix[:, base + k * LEAF : base + (k + 1) * LEAF]).astype(BF16)
            for i in range(NZ):
                if leaves == 1:
                    dst[ch, i] = part[:, i * UNIT : (i + 1) * UNIT]
                else:
                    dst[ch, k, i] = part[:, i * UNIT : (i + 1) * UNIT]

    def skip_columns(px, d):
        return m2[:, pl.ds(at(((xo if px else x) // 2 * NZ + zm(d)) * UNIT), UNIT)]

    def solve2(ch):
        total = y2[ch] - nt(u1b[ch], skip_columns(0, 0))
        copies = gather_skip("u1", u1b, u1r, ch)
        for i, (px, d) in reversed(list(enumerate(PAIR_PEERS))):
            copies[i].wait_recv()
            total -= nt(u1r[ch, i], skip_columns(px, d))
        part = total.astype(BF16)
        for k in range(NX):
            s2rs[ch, k] = part[:, k * UNIT : (k + 1) * UNIT]
        start(reduce_x("s2r", s2rs, s2rr, ch))

    chains(solve2)

    def summed(copies, own, dst, ch):
        total = own.astype(F32)
        for i in reversed(range(len(copies))):
            copies[i].wait_recv()
            total += dst[ch, i].astype(F32)
        return total

    def share2(ch):
        s2b[ch] = summed(reduce_x("s2r", s2rs, s2rr, ch), s2rs[ch, x], s2rr, ch).astype(BF16)
        start(gather_x("s2a", s2b, s2ar, ch))

    chains(share2)
    sent(swaps + r0_same + r0_cross + blocks + hands + t_z + t_x + r1_x + r1_z + r2_z)

    def row_block(matrix, index, first, count):
        return matrix[pl.ds(at(index * UNIT), UNIT), first : first + count]

    def fetch2(ch):
        copies = gather_x("s2a", s2b, s2ar, ch)
        totals = [nn(s2b[ch], row_block(m2, x, side * LEAF, LEAF)) for side in range(2)]
        for i, d in reversed(list(enumerate(X_PEERS))):
            copies[i].wait_recv()
            for side in range(2):
                totals[side] += nn(s2ar[ch, i], row_block(m2, xm(d), side * LEAF, LEAF))
        for side in range(2):
            part = totals[side].astype(BF16)
            for i in range(NZ):
                f1s[ch, side, i] = part[:, i * UNIT : (i + 1) * UNIT]
        start(reduce_skip("f1", f1s, f1r, ch))

    chains(fetch2)

    def sent_forward(ch):
        sent(gather_z("a1", s0b, a1r, ch))
        sent(gather_pair("u0", u0b, u0r, ch))
        sent(gather_pair("s1", s1b, s1r, ch))
        sent(gather_skip("u1", u1b, u1r, ch))
        sent(reduce_x("s2r", s2rs, s2rr, ch))
        sent(gather_x("s2a", s2b, s2ar, ch))

    chains(sent_forward)

    def back2(ch):
        total = nn(s2b[ch], row_block(d2, x, 0, LEAF))
        for i, d in enumerate(X_PEERS):
            total += nn(s2ar[ch, i], row_block(d2, xm(d), 0, LEAF))
        part = total.astype(BF16)
        for i in range(NZ):
            d2zs[ch, i] = part[:, i * UNIT : (i + 1) * UNIT]
        start(reduce_z("d2z", d2zs, d2zr, ch))

    def out_copies(level):
        keep = pltpu.make_async_copy(stage_own.at[level], out_hbm.at[level, :, mine], lsem.at[6 + level])
        hand = copy(stage_other.at[level], out_hbm.at[level, :, mine], SEM_AT["out"] + level, core)
        return keep, hand

    def finish(level, name, src, dst):
        def one(ch):
            sol[level, cols(ch), :] = summed(reduce_z(name, src, dst, ch), src[ch, z], dst, ch)

        chains(one)
        stage_other[level] = sol[level, :, theirs].T
        keep, hand = out_copies(level)
        hand.start()
        stage_own[level] = sol[level, :, mine].T
        keep.start()

    def fetch1(ch):
        fetched = summed(reduce_skip("f1", f1s, f1r, ch), f1s[ch, x // 2, z], f1r, ch).astype(BF16)
        spread(em, E_AT[1], fetched, e1s, ch, 2)
        start(reduce_pair("e1", e1s, e1r, ch))

    chains(fetch1)

    def weigh1(ch):
        carried = summed(reduce_pair("e1", e1s, e1r, ch), e1s[ch, xpar, z], e1r, ch)
        weights = (s1b[ch].astype(F32) - carried).astype(BF16)
        w1b[ch] = weights
        spread(m1, 0, weights, f0s, ch, 2)
        start(reduce_pair("f0", f0s, f0r, ch))

    chains(weigh1)
    chains(back2)

    def back1(ch):
        spread(dm, D_AT[1], w1b[ch], d1xs, ch, 2)
        start(x_pair("d1x", d1xs, d1xr, ch))

    chains(back1)

    def fetch0(ch):
        fetched = summed(reduce_pair("f0", f0s, f0r, ch), f0s[ch, xpar, z], f0r, ch).astype(BF16)
        spread(em, E_AT[0], fetched, w0s, ch, 1)
        start(reduce_z("w0", w0s, w0r, ch))

    chains(fetch0)
    finish(2, "d2z", d2zs, d2zr)

    def back1z(ch):
        received(x_pair("d1x", d1xs, d1xr, ch))
        for k in range(NZ):
            d1zs[ch, k] = (d1xs[ch, xpar, k].astype(F32) + d1xr[ch, 0, k].astype(F32)).astype(BF16)
        start(reduce_z("d1z", d1zs, d1zr, ch))

    chains(back1z)

    def weigh0(ch):
        carried = summed(reduce_z("w0", w0s, w0r, ch), w0s[ch, z], w0r, ch)
        weights = (s0b[ch].astype(F32) - carried).astype(BF16)
        spread(dm, D_AT[0], weights, l0s, ch, 1)
        start(reduce_z("l0", l0s, l0r, ch))

    chains(weigh0)

    def sent_adjoint(ch):
        sent(reduce_skip("f1", f1s, f1r, ch))
        sent(reduce_z("d2z", d2zs, d2zr, ch))
        sent(reduce_pair("e1", e1s, e1r, ch))
        sent(reduce_pair("f0", f0s, f0r, ch))
        sent(x_pair("d1x", d1xs, d1xr, ch))
        sent(reduce_z("w0", w0s, w0r, ch))

    chains(sent_adjoint)
    finish(1, "d1z", d1zs, d1zr)

    finish(0, "l0", l0s, l0r)

    def sent_last(ch):
        sent(reduce_z("d1z", d1zs, d1zr, ch))
        sent(reduce_z("l0", l0s, l0r, ch))

    chains(sent_last)
    for level in range(3):
        keep, hand = out_copies(level)
        keep.wait()
        hand.wait()


def shards(rhs, inverse_blocks, update_blocks, asm_owner, asm_row):
    k, w = CHAINS, WIDTH
    hbm = pl.BlockSpec(memory_space=pl.ANY)
    block = lambda *lead: pltpu.VMEM((k, *lead, w, UNIT), BF16)
    return pl.pallas_call(
        kernel,
        out_shape=jax.ShapeDtypeStruct(rhs.shape, F32),
        in_specs=[hbm] * 5,
        out_specs=hbm,
        scratch_shapes=[
            pltpu.VMEM((2, 1, ROW), jnp.int32),
            pltpu.VMEM((2, ROW), jnp.int32),
            pltpu.VMEM((3, ROW, 2 * HALF), BF16),
            pltpu.VMEM((UNIT, 3 * LEAF), BF16),
            pltpu.VMEM((LEAF, LEAF), BF16),
            pltpu.VMEM((UNIT, 3 * LEAF), BF16),
            pltpu.VMEM((UNIT, 2 * LEAF), BF16),
            pltpu.VMEM((LEAF, 2 * LEAF), BF16),
            pltpu.VMEM((3, HALF, ROW), BF16),
            pltpu.VMEM((3, HALF, UNIT), BF16),
            pltpu.VMEM((NX, NZ, 8, UNIT), jnp.int32),
            pltpu.VMEM((2, NZ, HALF, UNIT), BF16),
            pltpu.VMEM((NZ, HALF, UNIT), BF16),
            pltpu.VMEM((LEAF, UNIT), BF16),
            block(), block(), block(), block(), block(), block(),
            pltpu.VMEM((NZ, HALF, UNIT), BF16),
            block(3), block(7), block(7), block(7),
            pltpu.VMEM((k, w, UNIT), F32),
            pltpu.VMEM((k, w, LEAF), F32),
            block(4), block(3), block(3),
            block(2, 4), block(7), block(2, 4), block(7), block(2, 4), block(7),
            block(4), block(3), block(4), block(3),
            block(4), block(3),
            block(2, 4), block(1, 4), block(4), block(3),
            pltpu.VMEM((3, HALF, UNIT), F32),
            pltpu.VMEM((3, ROW, HALF), F32),
            pltpu.VMEM((3, ROW, HALF), F32),
            pltpu.SemaphoreType.DMA((SEM_COUNT,)),
            pltpu.SemaphoreType.DMA((SEM_COUNT,)),
            pltpu.SemaphoreType.DMA((13,)),
        ],
        compiler_params=pltpu.CompilerParams(collective_id=0, has_side_effects=True, vmem_limit_bytes=32 * 2**20),
    )(*[pltpu.with_memory_space_constraint(one, pltpu.HBM) for one in (asm_owner.reshape(asm_row.shape[0], 1, asm_row.shape[1]), asm_row, rhs, inverse_blocks, update_blocks)])


def solution(mesh):
    placed = (
        P(None, ("leaf", "front"), None),
        P(("leaf", "front"), None),
        P(("leaf", "front"), None),
        P(None, ("leaf", "front"), None),
        P(None, ("leaf", "front")),
    )
    return jax.shard_map(
        shards, mesh=mesh, in_specs=placed, out_specs=P(None, ("leaf", "front"), None), check_vma=False
    )
```

```python
import functools

import jax
import jax.numpy as jnp
from jax import lax
from jax.experimental import pallas as pl
from jax.experimental.pallas import tpu as pltpu
from jax.sharding import PartitionSpec as P

MESH = pl.DeviceIdType.MESH
F32, BF16 = jnp.float32, jnp.bfloat16

CHAINS = 2
ROW = 128
UNIT = 256
HALF = 128
NX, NZ = 4, 4
LEAF = UNIT * NZ
WIDTH = HALF // CHAINS
D_AT = (0, LEAF)
E_AT = (0, LEAF)

Z_PEERS = (2, 1, 3)
PAIR_PEERS = ((1, 2), (1, 1), (1, 3), (0, 2), (1, 0), (0, 1), (0, 3))
X_PEERS = (2, 1, 3)
QUAD_PEERS = tuple((dx, dz) for dx in (2, 1, 3, 0) for dz in (2, 1, 3, 0) if dx or dz)

CHAINED = (
    ("a1", 3), ("u0", 7), ("s1", 7), ("u1", 7), ("s2r", 3), ("s2a", 3), ("f1", 7), ("e1", 7), ("f0", 7),
    ("w0", 3), ("l0", 3), ("d2z", 3), ("d1x", 1), ("d1z", 3),
)
SINGLE = (("a0", 3), ("a0x", 3), ("core", 9), ("block", 3), ("hand", 3), ("tz", 3), ("tx", 3), ("r1z", 3), ("r1x", 1), ("r2z", 3), ("out", 3))
SEM_AT, SEM_COUNT = {}, 0
for _name, _n in CHAINED:
    SEM_AT[_name] = SEM_COUNT
    SEM_COUNT += _n * CHAINS
for _name, _n in SINGLE:
    SEM_AT[_name] = SEM_COUNT
    SEM_COUNT += _n


def nt(left, right):
    return lax.dot_general(left, right, (((1,), (1,)), ((), ())), preferred_element_type=F32)


def nn(left, right):
    return lax.dot_general(left, right, (((1,), (0,)), ((), ())), preferred_element_type=F32)


def kernel(
    owner_hbm, row_hbm, rhs_hbm, d_hbm, e_hbm, out_hbm,
    owner_ref, row_ref, rhs_v, dm, d2, em, m1, m2, swap, rt, tg, zr1, zr2, select,
    s0b, u0b, s1b, u1b, s2b, w1b,
    a0, a1r, u0r, s1r, u1r, y1, y2, s2rs, s2rr, s2ar,
    f1s, f1r, e1s, e1r, f0s, f0r, w0s, w0r, l0s, l0r,
    d2zs, d2zr, d1xs, d1xr, d1zs, d1zr,
    sol, stage_own, stage_other,
    ssem, rsem, lsem,
):
    leaf, front = lax.axis_index("leaf"), lax.axis_index("front")
    x, y = lax.rem(leaf, NX), leaf // NX
    z, c = front // 2, lax.rem(front, 2)
    other = 1 - c
    xp = x + 1 - 2 * lax.rem(x, 2)
    xpar = lax.rem(x, 2)
    xo = lax.rem(x + 2, NX)

    def dev(xx, zz):
        return (y * NX + xx, zz * 2 + c)

    core = (leaf, z * 2 + other)

    def dev_other(zz):
        return (leaf, zz * 2 + other)

    def zp(d):
        return lax.rem(z + d, NZ)

    def zm(d):
        return lax.rem(z + NZ - d, NZ)

    def xq(d):
        return lax.rem(x + d, NX)

    def xm(d):
        return lax.rem(x + NX - d, NX)

    def at(value):
        return pl.multiple_of(value, UNIT)

    def copy(src, dst, sem, device):
        return pltpu.make_async_remote_copy(
            src_ref=src, dst_ref=dst, send_sem=ssem.at[sem], recv_sem=rsem.at[sem], device_id=device, device_id_type=MESH
        )

    def chains(body):
        def step(ch, carry):
            body(ch)
            return carry

        lax.fori_loop(0, CHAINS, step, 0)

    def cols(ch):
        return pl.ds(pl.multiple_of(ch * WIDTH, WIDTH), WIDTH)

    def gather_z(name, src, dst, ch):
        return [copy(src.at[ch], dst.at[ch, i], SEM_AT[name] + ch * 3 + i, dev(x, zp(d))) for i, d in enumerate(Z_PEERS)]

    def gather_pair(name, src, dst, ch):
        return [
            copy(src.at[ch], dst.at[ch, i], SEM_AT[name] + ch * 7 + i, dev(xp if px else x, zp(d)))
            for i, (px, d) in enumerate(PAIR_PEERS)
        ]

    def gather_skip(name, src, dst, ch):
        return [
            copy(src.at[ch], dst.at[ch, i], SEM_AT[name] + ch * 7 + i, dev(xo if px else x, zp(d)))
            for i, (px, d) in enumerate(PAIR_PEERS)
        ]

    def gather_x(name, src, dst, ch):
        return [copy(src.at[ch], dst.at[ch, i], SEM_AT[name] + ch * 3 + i, dev(xq(d), z)) for i, d in enumerate(X_PEERS)]

    def reduce_z(name, src, dst, ch):
        return [
            copy(src.at[ch, zp(d)], dst.at[ch, i], SEM_AT[name] + ch * 3 + i, dev(x, zp(d))) for i, d in enumerate(Z_PEERS)
        ]

    def reduce_pair(name, src, dst, ch):
        out = []
        for i, (px, d) in enumerate(PAIR_PEERS):
            xx = xp if px else x
            out.append(copy(src.at[ch, lax.rem(xx, 2), zp(d)], dst.at[ch, i], SEM_AT[name] + ch * 7 + i, dev(xx, zp(d))))
        return out

    def reduce_skip(name, src, dst, ch):
        out = []
        for i, (px, d) in enumerate(PAIR_PEERS):
            xx = xo if px else x
            out.append(copy(src.at[ch, xx // 2, zp(d)], dst.at[ch, i], SEM_AT[name] + ch * 7 + i, dev(xx, zp(d))))
        return out

    def reduce_x(name, src, dst, ch):
        return [copy(src.at[ch, xq(d)], dst.at[ch, i], SEM_AT[name] + ch * 3 + i, dev(xq(d), z)) for i, d in enumerate(X_PEERS)]

    def x_pair(name, src, dst, ch):
        return [copy(src.at[ch, 1 - xpar], dst.at[ch, 0], SEM_AT[name] + ch, dev(xp, z))]

    def start(copies):
        for one in copies:
            one.start()

    def received(copies):
        for one in copies:
            one.wait_recv()

    def sent(copies):
        for one in copies:
            one.wait_send()

    mine, theirs = pl.ds(pl.multiple_of(c * ROW, ROW), ROW), pl.ds(pl.multiple_of(other * ROW, ROW), ROW)
    spans = ((d_hbm, dm, 0, LEAF), (e_hbm, em, 0, LEAF), (d_hbm, dm, LEAF, 2 * LEAF), (e_hbm, em, LEAF, 2 * LEAF))

    def d2_columns(leaf_x):
        return d_hbm.at[:, pl.ds(pl.multiple_of((3 + leaf_x) * LEAF, LEAF), LEAF)]

    def d2_rows(leaf_x):
        return d2.at[pl.ds(pl.multiple_of(leaf_x * UNIT + c * ROW, ROW), ROW)]

    load_rhs = [pltpu.make_async_copy(rhs_hbm.at[level], rhs_v.at[level], lsem.at[9 + level]) for level in range(3)]
    load_lists = [
        pltpu.make_async_copy(owner_hbm, owner_ref, lsem.at[12]), pltpu.make_async_copy(row_hbm, row_ref, lsem.at[0])
    ]
    for one in load_rhs + load_lists:
        one.start()
    loads = [
        pltpu.make_async_copy(src.at[:, pl.ds(a, n)], dst.at[mine, pl.ds(a, n)], lsem.at[1 + i])
        for i, (src, dst, a, n) in enumerate(spans)
    ]
    loads.append(pltpu.make_async_copy(d2_columns(x), d2_rows(x), lsem.at[5]))
    for one in loads:
        one.start()
    barrier = pltpu.get_barrier_semaphore()
    pl.semaphore_signal(barrier, inc=1, device_id=core, device_id_type=MESH)
    for dx, d in QUAD_PEERS:
        pl.semaphore_signal(barrier, inc=1, device_id=dev(xq(dx), zp(d)), device_id_type=MESH)
    for d in Z_PEERS:
        pl.semaphore_signal(barrier, inc=1, device_id=dev_other(zp(d)), device_id_type=MESH)

    def turn(level, own):
        load_rhs[level].wait()
        swap[level] = rhs_v[level, :, theirs].astype(F32).T.astype(BF16)
        own[:, mine] = rhs_v[level, :, mine].astype(F32).T.astype(BF16)

    turn(0, a0.at[0])
    pl.semaphore_wait(barrier, 19)
    half = a0.at[0, :, mine]
    r0_same = [copy(half, a0.at[d, :, mine], SEM_AT["a0"] + i, dev(x, zp(d))) for i, d in enumerate(Z_PEERS)]
    r0_cross = [copy(swap.at[0], a0.at[d, :, mine], SEM_AT["a0x"] + i, dev_other(zp(d))) for i, d in enumerate(Z_PEERS)]
    for i in range(3):
        r0_same[i].start()
        r0_cross[i].start()
    swaps = [copy(swap.at[0], half, SEM_AT["core"], core)]
    swaps += [copy(swap.at[level], rt.at[level, :, mine], SEM_AT["core"] + level, core) for level in (1, 2)]
    swaps.append(copy(tg.at[0, 0, :, mine], tg.at[0, 0, :, mine], SEM_AT["core"] + 3, core))
    swaps += [
        copy(src.at[:, pl.ds(a, n)], dst.at[mine, pl.ds(a, n)], SEM_AT["core"] + 4 + i, core)
        for i, (src, dst, a, n) in enumerate(spans)
    ]
    swaps.append(copy(d2_columns(x), d2_rows(x), SEM_AT["core"] + 8, core))
    swaps[0].start()
    swaps[4].start()
    turn(1, rt.at[1])
    swaps[1].start()
    swaps[5].start()

    for one in load_lists:
        one.wait()
    for level in range(2):
        owner = owner_ref[level]
        row = row_ref[level : level + 1, :]
        if level == 0:
            target = owner * ROW + row
        else:
            target = xpar * LEAF + (owner // 8) * (2 * LEAF) + lax.rem(owner, 8) * ROW + row
        tg[0, 0, level : level + 1, mine] = target
    swaps[3].start()
    turn(2, rt.at[2])
    swaps[2].start()
    for i in (6, 7, 8):
        swaps[i].start()

    t_z = [copy(tg.at[0, 0], tg.at[0, d], SEM_AT["tz"] + i, dev(x, zp(d))) for i, d in enumerate(Z_PEERS)]
    t_x = [copy(tg.at[0], tg.at[d], SEM_AT["tx"] + i, dev(xq(d), z)) for i, d in enumerate(Z_PEERS)]
    r1_x = [copy(rt.at[1], zr1.at[1, 0], SEM_AT["r1x"], dev(xp, z))]
    r1_z = [copy(zr1.at[:, 0], zr1.at[:, d], SEM_AT["r1z"] + i, dev(x, zp(d))) for i, d in enumerate(Z_PEERS)]
    r2_z = [copy(rt.at[2], zr2.at[d], SEM_AT["r2z"] + i, dev(x, zp(d))) for i, d in enumerate(Z_PEERS)]
    blocks = [copy(d2_columns(xq(d)), d2_rows(x), SEM_AT["block"] + i, dev(xq(d), z)) for i, d in enumerate(X_PEERS)]
    hands = [copy(d2_rows(xm(d)), d2_rows(xm(d)), SEM_AT["hand"] + i, core) for i, d in enumerate(X_PEERS)]
    swaps[3].wait_recv()
    start(t_z)
    swaps[1].wait_recv()
    start(r1_x)
    start(blocks[1:])
    zr1[0, 0] = rt[1]

    def d_block(level, index):
        return dm[:, pl.ds(at(D_AT[level] + index * UNIT), UNIT)]

    def e_block(level, index):
        return em[:, pl.ds(at(E_AT[level] + index * UNIT), UNIT)]

    def pair_index(px, d):
        return lax.rem(xp if px else x, 2) * NZ + zm(d)

    loads[0].wait()
    swaps[4].wait_recv()

    def solve0(ch):
        total = nt(a0[0, cols(ch), :], d_block(0, z))
        for d in range(1, NZ):
            total += nt(a0[d, cols(ch), :], d_block(0, zm(d)))
        s0b[ch] = total.astype(BF16)
        start(gather_z("a1", s0b, a1r, ch))

    swaps[0].wait_recv()
    received(r0_same + r0_cross)
    chains(solve0)
    start(blocks[:1])

    received(t_z)
    start(t_x)
    received(r1_x)
    start(r1_z)

    def fill_select(target, base, count):
        for k in range(count):
            rows = lax.broadcasted_iota(jnp.int32, (UNIT, UNIT), 0) + (base + k * UNIT)
            select[k * UNIT : (k + 1) * UNIT, :] = jnp.where(rows == target, 1.0, 0.0).astype(BF16)

    def select1(j, carry):
        px, d = j // NZ, lax.rem(j, NZ)
        dx = px * (3 - 2 * xpar)
        source = lax.rem(x + px, 2) * NZ + zm(d)
        target = tg[dx, d, 0:1, :]
        total = jnp.zeros((UNIT, UNIT), F32)
        for part in range(2):
            fill_select(target, part * LEAF, 4)
            total += nn(dm[:, D_AT[1] + part * LEAF : D_AT[1] + (part + 1) * LEAF], select[...])
        m1[:, pl.ds(at(source * UNIT), UNIT)] = total.astype(BF16)
        return carry

    loads[2].wait()
    swaps[6].wait_recv()
    lax.fori_loop(0, 3, select1, 0)
    loads[1].wait()
    swaps[5].wait_recv()

    def update0(ch):
        total = nt(s0b[ch], e_block(0, z))
        copies = gather_z("a1", s0b, a1r, ch)
        for i, d in enumerate(Z_PEERS):
            copies[i].wait_recv()
            total += nt(a1r[ch, i], e_block(0, zm(d)))
        u0b[ch] = total.astype(BF16)
        start(gather_pair("u0", u0b, u0r, ch))

    chains(update0)

    received(t_x)

    lax.fori_loop(3, 2 * NZ, select1, 0)
    received(r1_z)

    def rhs1(ch):
        total = jnp.zeros((WIDTH, UNIT), F32)
        for px in range(2):
            for d in range(NZ):
                total += nt(zr1[px, d, cols(ch), :], d_block(1, pair_index(px, d)))
        y1[ch] = total

    chains(rhs1)

    def solve1(ch):
        total = nt(u0b[ch], m1[:, pl.ds(at((xpar * NZ + z) * UNIT), UNIT)])
        copies = gather_pair("u0", u0b, u0r, ch)
        for i, (px, d) in reversed(list(enumerate(PAIR_PEERS))):
            copies[i].wait_recv()
            total += nt(u0r[ch, i], m1[:, pl.ds(at(pair_index(px, d) * UNIT), UNIT)])
        s1b[ch] = (y1[ch] - total).astype(BF16)
        start(gather_pair("s1", s1b, s1r, ch))

    chains(solve1)

    swaps[2].wait_recv()
    start(r2_z)
    for i in range(3):
        blocks[i].wait_recv()
        hands[i].start()
    loads[4].wait()
    swaps[8].wait_recv()
    received(hands)

    def select2(j, carry):
        side, zz = j // NZ, lax.rem(j, NZ)
        dx = lax.rem(x // 2 + side, 2) * 2
        target = tg[dx, lax.rem(z + NZ - zz, NZ), 1:2, :]
        fill_select(target, x * LEAF, 4)
        m2[:, pl.ds(at(j * UNIT), UNIT)] = nn(d2[...], select[...]).astype(BF16)
        return carry

    lax.fori_loop(0, 5, select2, 0)

    loads[3].wait()
    swaps[7].wait_recv()

    def update1(ch):
        total = nt(s1b[ch], e_block(1, xpar * NZ + z))
        copies = gather_pair("s1", s1b, s1r, ch)
        for i, (px, d) in reversed(list(enumerate(PAIR_PEERS))):
            copies[i].wait_recv()
            total += nt(s1r[ch, i], e_block(1, pair_index(px, d)))
        u1b[ch] = total.astype(BF16)
        start(gather_skip("u1", u1b, u1r, ch))

    chains(update1)

    lax.fori_loop(5, 8, select2, 0)
    received(r2_z)

    def rhs2(ch):
        total = nt(rt[2, cols(ch), :], d2[:, pl.ds(at(z * UNIT), UNIT)])
        for d in range(1, NZ):
            total += nt(zr2[d, cols(ch), :], d2[:, pl.ds(at(zm(d) * UNIT), UNIT)])
        y2[ch] = total

    chains(rhs2)

    def spread(matrix, base, vector, dst, ch, leaves):
        for k in range(leaves):
            part = nn(vector, matrix[:, base + k * LEAF : base + (k + 1) * LEAF]).astype(BF16)
            for i in range(NZ):
                if leaves == 1:
                    dst[ch, i] = part[:, i * UNIT : (i + 1) * UNIT]
                else:
                    dst[ch, k, i] = part[:, i * UNIT : (i + 1) * UNIT]

    def skip_columns(px, d):
        return m2[:, pl.ds(at(((xo if px else x) // 2 * NZ + zm(d)) * UNIT), UNIT)]

    def solve2(ch):
        total = y2[ch] - nt(u1b[ch], skip_columns(0, 0))
        copies = gather_skip("u1", u1b, u1r, ch)
        for i, (px, d) in reversed(list(enumerate(PAIR_PEERS))):
            copies[i].wait_recv()
            total -= nt(u1r[ch, i], skip_columns(px, d))
        part = total.astype(BF16)
        for k in range(NX):
            s2rs[ch, k] = part[:, k * UNIT : (k + 1) * UNIT]
        start(reduce_x("s2r", s2rs, s2rr, ch))

    chains(solve2)

    def summed(copies, own, dst, ch):
        total = own.astype(F32)
        for i in reversed(range(len(copies))):
            copies[i].wait_recv()
            total += dst[ch, i].astype(F32)
        return total

    def share2(ch):
        s2b[ch] = summed(reduce_x("s2r", s2rs, s2rr, ch), s2rs[ch, x], s2rr, ch).astype(BF16)
        start(gather_x("s2a", s2b, s2ar, ch))

    chains(share2)
    sent(swaps + r0_same + r0_cross + blocks + hands + t_z + t_x + r1_x + r1_z + r2_z)

    def row_block(matrix, index, first, count):
        return matrix[pl.ds(at(index * UNIT), UNIT), first : first + count]

    def fetch2(ch):
        copies = gather_x("s2a", s2b, s2ar, ch)
        totals = [nn(s2b[ch], row_block(m2, x, side * LEAF, LEAF)) for side in range(2)]
        for i, d in reversed(list(enumerate(X_PEERS))):
            copies[i].wait_recv()
            for side in range(2):
                totals[side] += nn(s2ar[ch, i], row_block(m2, xm(d), side * LEAF, LEAF))
        for side in range(2):
            part = totals[side].astype(BF16)
            for i in range(NZ):
                f1s[ch, side, i] = part[:, i * UNIT : (i + 1) * UNIT]
        start(reduce_skip("f1", f1s, f1r, ch))

    chains(fetch2)

    def sent_forward(ch):
        sent(gather_z("a1", s0b, a1r, ch))
        sent(gather_pair("u0", u0b, u0r, ch))
        sent(gather_pair("s1", s1b, s1r, ch))
        sent(gather_skip("u1", u1b, u1r, ch))
        sent(reduce_x("s2r", s2rs, s2rr, ch))
        sent(gather_x("s2a", s2b, s2ar, ch))

    chains(sent_forward)

    def back2(ch):
        total = nn(s2b[ch], row_block(d2, x, 0, LEAF))
        for i, d in enumerate(X_PEERS):
            total += nn(s2ar[ch, i], row_block(d2, xm(d), 0, LEAF))
        part = total.astype(BF16)
        for i in range(NZ):
            d2zs[ch, i] = part[:, i * UNIT : (i + 1) * UNIT]
        start(reduce_z("d2z", d2zs, d2zr, ch))

    def out_copies(level):
        keep = pltpu.make_async_copy(stage_own.at[level], out_hbm.at[level, :, mine], lsem.at[6 + level])
        hand = copy(stage_other.at[level], out_hbm.at[level, :, mine], SEM_AT["out"] + level, core)
        return keep, hand

    def finish(level, name, src, dst):
        def one(ch):
            sol[level, cols(ch), :] = summed(reduce_z(name, src, dst, ch), src[ch, z], dst, ch)

        chains(one)
        stage_other[level] = sol[level, :, theirs].T
        keep, hand = out_copies(level)
        hand.start()
        stage_own[level] = sol[level, :, mine].T
        keep.start()

    def fetch1(ch):
        fetched = summed(reduce_skip("f1", f1s, f1r, ch), f1s[ch, x // 2, z], f1r, ch).astype(BF16)
        spread(em, E_AT[1], fetched, e1s, ch, 2)
        start(reduce_pair("e1", e1s, e1r, ch))

    chains(fetch1)

    def weigh1(ch):
        carried = summed(reduce_pair("e1", e1s, e1r, ch), e1s[ch, xpar, z], e1r, ch)
        weights = (s1b[ch].astype(F32) - carried).astype(BF16)
        w1b[ch] = weights
        spread(m1, 0, weights, f0s, ch, 2)
        start(reduce_pair("f0", f0s, f0r, ch))

    chains(weigh1)
    chains(back2)

    def back1(ch):
        spread(dm, D_AT[1], w1b[ch], d1xs, ch, 2)
        start(x_pair("d1x", d1xs, d1xr, ch))

    chains(back1)

    def fetch0(ch):
        fetched = summed(reduce_pair("f0", f0s, f0r, ch), f0s[ch, xpar, z], f0r, ch).astype(BF16)
        spread(em, E_AT[0], fetched, w0s, ch, 1)
        start(reduce_z("w0", w0s, w0r, ch))

    chains(fetch0)
    finish(2, "d2z", d2zs, d2zr)

    def back1z(ch):
        received(x_pair("d1x", d1xs, d1xr, ch))
        for k in range(NZ):
            d1zs[ch, k] = (d1xs[ch, xpar, k].astype(F32) + d1xr[ch, 0, k].astype(F32)).astype(BF16)
        start(reduce_z("d1z", d1zs, d1zr, ch))

    chains(back1z)

    def weigh0(ch):
        carried = summed(reduce_z("w0", w0s, w0r, ch), w0s[ch, z], w0r, ch)
        weights = (s0b[ch].astype(F32) - carried).astype(BF16)
        spread(dm, D_AT[0], weights, l0s, ch, 1)
        start(reduce_z("l0", l0s, l0r, ch))

    chains(weigh0)

    def sent_adjoint(ch):
        sent(reduce_skip("f1", f1s, f1r, ch))
        sent(reduce_z("d2z", d2zs, d2zr, ch))
        sent(reduce_pair("e1", e1s, e1r, ch))
        sent(reduce_pair("f0", f0s, f0r, ch))
        sent(x_pair("d1x", d1xs, d1xr, ch))
        sent(reduce_z("w0", w0s, w0r, ch))

    chains(sent_adjoint)
    finish(1, "d1z", d1zs, d1zr)

    finish(0, "l0", l0s, l0r)

    def sent_last(ch):
        sent(reduce_z("d1z", d1zs, d1zr, ch))
        sent(reduce_z("l0", l0s, l0r, ch))

    chains(sent_last)
    for level in range(3):
        keep, hand = out_copies(level)
        keep.wait()
        hand.wait()


def shards(rhs, inverse_blocks, update_blocks, asm_owner, asm_row):
    k, w = CHAINS, WIDTH
    hbm = pl.BlockSpec(memory_space=pl.ANY)
    block = lambda *lead: pltpu.VMEM((k, *lead, w, UNIT), BF16)
    return pl.pallas_call(
        kernel,
        out_shape=jax.ShapeDtypeStruct(rhs.shape, F32),
        in_specs=[hbm] * 5,
        out_specs=hbm,
        scratch_shapes=[
            pltpu.VMEM((2, 1, ROW), jnp.int32),
            pltpu.VMEM((2, ROW), jnp.int32),
            pltpu.VMEM((3, ROW, 2 * HALF), BF16),
            pltpu.VMEM((UNIT, 3 * LEAF), BF16),
            pltpu.VMEM((LEAF, LEAF), BF16),
            pltpu.VMEM((UNIT, 3 * LEAF), BF16),
            pltpu.VMEM((UNIT, 2 * LEAF), BF16),
            pltpu.VMEM((LEAF, 2 * LEAF), BF16),
            pltpu.VMEM((3, HALF, ROW), BF16),
            pltpu.VMEM((3, HALF, UNIT), BF16),
            pltpu.VMEM((NX, NZ, 8, UNIT), jnp.int32),
            pltpu.VMEM((2, NZ, HALF, UNIT), BF16),
            pltpu.VMEM((NZ, HALF, UNIT), BF16),
            pltpu.VMEM((LEAF, UNIT), BF16),
            block(), block(), block(), block(), block(), block(),
            pltpu.VMEM((NZ, HALF, UNIT), BF16),
            block(3), block(7), block(7), block(7),
            pltpu.VMEM((k, w, UNIT), F32),
            pltpu.VMEM((k, w, LEAF), F32),
            block(4), block(3), block(3),
            block(2, 4), block(7), block(2, 4), block(7), block(2, 4), block(7),
            block(4), block(3), block(4), block(3),
            block(4), block(3),
            block(2, 4), block(1, 4), block(4), block(3),
            pltpu.VMEM((3, HALF, UNIT), F32),
            pltpu.VMEM((3, ROW, HALF), F32),
            pltpu.VMEM((3, ROW, HALF), F32),
            pltpu.SemaphoreType.DMA((SEM_COUNT,)),
            pltpu.SemaphoreType.DMA((SEM_COUNT,)),
            pltpu.SemaphoreType.DMA((13,)),
        ],
        compiler_params=pltpu.CompilerParams(collective_id=0, has_side_effects=True, vmem_limit_bytes=32 * 2**20),
    )(*[pltpu.with_memory_space_constraint(one, pltpu.HBM) for one in (asm_owner.reshape(asm_row.shape[0], 1, asm_row.shape[1]), asm_row, rhs, inverse_blocks, update_blocks)])


def solution(mesh):
    placed = (
        P(None, ("leaf", "front"), None),
        P(("leaf", "front"), None),
        P(("leaf", "front"), None),
        P(None, ("leaf", "front"), None),
        P(None, ("leaf", "front")),
    )
    return jax.shard_map(
        shards, mesh=mesh, in_specs=placed, out_specs=P(None, ("leaf", "front"), None), check_vma=False
    )
```
